32 devices in a mesh: row: 4 (over z), col: 8 (over y, x, core).
Axes of the slice: x: 2, y: 2, z: 4, core: 2. Of those that a mesh axis runs over, the one named last changes fastest.
Arguments:
- image: float32 [16, 16, 64, 128], P('row', 'col'), may hold values from -6 to 6
- u_factors: bfloat16 [20, 16, 1024, 256], P('row', 'col'), may hold values from -0.125 to 0.125
- v_factors: bfloat16 [20, 16, 1024, 256], P('row', 'col'), may hold values from -0.1875 to 0.1875
- ranks: int32 [20, 16], P('row', 'col'), may hold values from 16 to 256
- measured: bfloat16 [20480, 128], P('row'), may hold values from -6 to 6
Outputs:
- new_image: float32 [16, 16, 64, 128], P('row', 'col')
The draws below stay inside these ranges and needn't reach their ends.
All inputs are finite; a program needn't handle non-finite values.
Results may differ from the reference program's by a relative error of at most 0.0051.
Values may be sent and summed in bfloat16 or wider, within the bound.
No kernel may reach another device: no remote copies, remote signals or barrier semaphores. Data moves between devices by JAX's collectives and lax.ppermute only.
A program may use at most 128 MiB of HBM per device.

```python
import jax
import jax.numpy as jnp
from jax import lax

TILE = 1024
RMAX = 256
F = 128
GZ = 64
GX = 16
GY = 16
COL_TILES = 16
ROW_TILES = 20
SAMPLES = 20480
N_COL = 8


def touch_ends(drawn, own_key, least, largest):
    longest = drawn.shape.index(max(drawn.shape))
    spots = []
    for shift in (0, 1):
        where = [jax.random.randint(jax.random.fold_in(own_key, axis), (), 0, length) for axis, length in enumerate(drawn.shape)]
        where[longest] = (where[longest] + shift) % drawn.shape[longest]
        spots.append(tuple(where))
    return drawn.at[spots[0]].set(least).at[spots[1]].set(largest)


def shard_levels(stream_key, extent, pieces, smallest, top_value):
    gain = 1.0
    for position, shards_of in pieces:
        steps = jax.random.uniform(jax.random.fold_in(jax.random.fold_in(stream_key, 6), position), (shards_of,), jnp.float32, smallest / len(pieces), top_value / len(pieces))
        gain = gain * jnp.repeat(jnp.exp(steps), extent[position] // shards_of).reshape((-1,) + (1,) * (len(extent) - 1 - position))
    return gain


def bell_draw(key, extent, scale, bound, cuts=(), kind=jnp.bfloat16):
    drawn = jax.random.normal(key, extent, jnp.float32) * scale
    if len(cuts) > 0:
        drawn = shard_levels(key, extent, cuts, -0.22, 0.18) * drawn
    return jnp.clip(drawn, min=-bound, max=bound).astype(kind)


def setup_inputs(seed: int = 0) -> dict:
    key_of = jax.random.split(jax.random.key(seed), 6)
    return {
        "image": bell_draw(key_of[0], (GX, GY, GZ, F), 1.0, 6.0, ((0, 4), (1, 8)), jnp.float32),
        "u_factors": bell_draw(key_of[1], (ROW_TILES, COL_TILES, TILE, RMAX), (RMAX * COL_TILES // 2) ** -0.5, 0.125, ((0, 4), (1, 8))),
        "v_factors": bell_draw(key_of[2], (ROW_TILES, COL_TILES, TILE, RMAX), TILE ** -0.5, 0.1875, ((0, 4), (1, 8))),
        "ranks": touch_ends(jax.random.randint(key_of[3], (ROW_TILES, COL_TILES), RMAX // 16, RMAX + 1), jax.random.fold_in(key_of[3], 1), RMAX // 16, RMAX).astype(jnp.int32),
        "measured": bell_draw(key_of[4], (SAMPLES, F), 1.0, 6.0, ((0, 4),)),
    }


diff_rate = 0.12
edge_scale = 0.5


def to_tiles(field):
    blocks = field.reshape(GX, N_COL, GY // N_COL, GZ, F)
    blocks = jnp.transpose(blocks, (1, 0, 2, 3, 4))
    return blocks.reshape(COL_TILES, TILE, F)


def from_tiles(tiles):
    blocks = tiles.reshape(N_COL, GX, GY // N_COL, GZ, F)
    blocks = jnp.transpose(blocks, (1, 0, 2, 3, 4))
    return blocks.reshape(GX, GY, GZ, F)


def flux(delta):
    scaled = delta / edge_scale
    return delta / (1.0 + scaled * scaled)


def diffuse_padded(padded):
    center = padded[1:-1, 1:-1, 1:-1]
    total = flux(padded[2:, 1:-1, 1:-1] - center) + flux(padded[:-2, 1:-1, 1:-1] - center)
    total = total + flux(padded[1:-1, 2:, 1:-1] - center) + flux(padded[1:-1, :-2, 1:-1] - center)
    total = total + flux(padded[1:-1, 1:-1, 2:] - center) + flux(padded[1:-1, 1:-1, :-2] - center)
    return center + diff_rate * total


def reference(image, u_factors, v_factors, ranks, measured):
    xtiles = to_tiles(image.astype(jnp.bfloat16)).astype(jnp.float32)
    mask = (jnp.arange(RMAX, dtype=jnp.int32)[None, None, :] < ranks[:, :, None]).astype(jnp.float32)

    def forward(items):
        u_row, v_row, m_row = items
        coef = jnp.einsum('jkr,jkf->jrf', v_row.astype(jnp.float32), xtiles) * m_row[:, :, None]
        coef = coef.astype(jnp.bfloat16).astype(jnp.float32)
        return jnp.einsum('jkr,jrf->kf', u_row.astype(jnp.float32), coef)

    predicted = lax.map(forward, (u_factors, v_factors, mask))
    resid = (predicted.reshape(SAMPLES, F) - measured.astype(jnp.float32)).astype(jnp.bfloat16)
    resid = resid.reshape(ROW_TILES, TILE, F).astype(jnp.float32)

    def adjoint(carry, items):
        u_row, v_row, m_row, r_row = items
        back = jnp.einsum('jkr,kf->jrf', u_row.astype(jnp.float32), r_row) * m_row[:, :, None]
        back = back.astype(jnp.bfloat16).astype(jnp.float32)
        return carry + jnp.einsum('jkr,jrf->jkf', v_row.astype(jnp.float32), back), None

    start = jnp.zeros((COL_TILES, TILE, F), jnp.float32)
    gradient, unused = lax.scan(adjoint, start, (u_factors, v_factors, mask, resid))
    moved = image - from_tiles(gradient)
    for step in range(2):
        moved = diffuse_padded(jnp.pad(moved, ((1, 1), (1, 1), (1, 1), (0, 0))))
    return moved
```

```python
import jax
import jax.numpy as jnp
from jax import lax
from jax.sharding import PartitionSpec as P

diff_rate = 0.12
edge_scale = 0.5


def swap(value, axis, distance):
    count = lax.axis_size(axis)
    return lax.ppermute(value, axis, [(i, i ^ distance) for i in range(count)])


def bits_of(count):
    bit = 1
    found = []
    while bit < count:
        found.append(bit)
        bit *= 2
    return found


def padded_2(block, sides, width):
    for axis, dim in sides:
        count = lax.axis_size(axis)
        forward = [(i, i + 1) for i in range(count - 1)]
        backward = [(target, source) for source, target in forward]
        low = lax.ppermute(
            lax.slice_in_dim(block, block.shape[dim] - width, None, axis=dim), axis, forward
        )
        high = lax.ppermute(lax.slice_in_dim(block, 0, width, axis=dim), axis, backward)
        block = jnp.concatenate([low, block, high], axis=dim)
    return block


def flux(delta):
    scaled = delta / edge_scale
    return delta / (1.0 + scaled * scaled)


def diffuse_margin(extended):
    padded = jnp.pad(extended, ((0, 0), (0, 0), (1, 1), (0, 0)))
    center = padded[1:-1, 1:-1, 1:-1]
    total = flux(padded[2:, 1:-1, 1:-1] - center) + flux(padded[:-2, 1:-1, 1:-1] - center)
    total = total + flux(padded[1:-1, 2:, 1:-1] - center) + flux(padded[1:-1, :-2, 1:-1] - center)
    total = total + flux(padded[1:-1, 1:-1, 2:] - center) + flux(padded[1:-1, 1:-1, :-2] - center)
    return center + diff_rate * total


def body(image, u_factors, v_factors, ranks, measured):
    row_tiles, col_tiles, tile_len, rank_max = u_factors.shape
    frames = image.shape[3]
    local_x, local_y = (image.shape[0], image.shape[1])
    rows, cols = lax.axis_size("row"), lax.axis_size("col")
    me_row, me_col = lax.axis_index("row"), lax.axis_index("col")

    have = {0: image.astype(jnp.bfloat16).reshape(-1, frames)}
    for bit in reversed(bits_of(rows)):
        for distance in list(have):
            have[distance ^ bit] = swap(have[distance], "row", bit)
    brick = have[0].shape[0]
    whole = jnp.zeros((rows * brick, frames), jnp.bfloat16)
    for distance, piece in have.items():
        whole = lax.dynamic_update_slice(whole, piece, ((me_row ^ distance) * brick, 0))
    xtiles = whole.reshape(col_tiles, tile_len, frames)

    levels = lax.broadcasted_iota(jnp.int32, (row_tiles, col_tiles, rank_max), 2)
    mask = (levels < ranks[:, :, None]).astype(jnp.float32)
    coef = jnp.einsum("ijkr,jkf->ijrf", v_factors, xtiles, preferred_element_type=jnp.float32)
    coef = (coef * mask[:, :, :, None]).astype(jnp.bfloat16)
    partial_value = jnp.einsum(
        "ijkr,ijrf->ikf", u_factors, coef, preferred_element_type=jnp.float32
    )
    part_len = tile_len // cols
    partial_value = partial_value.reshape(row_tiles, cols, part_len, frames)
    own = lambda distance: lax.dynamic_index_in_dim(
        partial_value, me_col ^ distance, axis=1, keepdims=False
    )
    evens = list(range(0, cols, 2))
    crossed = swap(jnp.stack([own(e + 1) for e in evens]).astype(jnp.bfloat16), "col", 1)
    chip = [own(e) + crossed[i].astype(jnp.float32) for i, e in enumerate(evens)]
    total = chip[0]
    for i, e in enumerate(evens[1:], 1):
        total = total + swap(chip[i].astype(jnp.bfloat16), "col", e).astype(jnp.float32)
    wanted = lax.dynamic_index_in_dim(
        measured.reshape(row_tiles, cols, part_len, frames), me_col, axis=1, keepdims=False
    )
    mine = (total - wanted.astype(jnp.float32)).astype(jnp.bfloat16)
    resid = jnp.zeros((row_tiles, tile_len, frames), jnp.bfloat16)
    for e in evens:
        piece = swap(mine, "col", e) if e else mine
        other = swap(piece, "col", 1)
        resid = lax.dynamic_update_slice(resid, piece, (0, (me_col ^ e) * part_len, 0))
        resid = lax.dynamic_update_slice(resid, other, (0, (me_col ^ (e + 1)) * part_len, 0))

    back = jnp.einsum("ijkr,ikf->ijrf", u_factors, resid, preferred_element_type=jnp.float32)
    back = (back * mask[:, :, :, None]).astype(jnp.bfloat16)
    grad_terms = jnp.einsum("ijkr,ijrf->jkf", v_factors, back, preferred_element_type=jnp.float32)
    grad_terms = grad_terms.reshape(rows, brick, frames)
    part = {
        distance: lax.dynamic_index_in_dim(grad_terms, me_row ^ distance, axis=0, keepdims=False)
        for distance in range(rows)
    }
    for bit in bits_of(rows):
        part = {
            d: part[d] + swap(part[d ^ bit].astype(jnp.bfloat16), "row", bit).astype(jnp.float32)
            for d in part
            if not d & bit
        }
    moved = image - part[0].reshape(image.shape)
    extended = padded_2(moved, (("row", 0), ("col", 1)), 2)
    middle = diffuse_margin(extended)
    grid_x = local_x * rows
    grid_y = local_y * cols
    pos_x = lax.broadcasted_iota(jnp.int32, (local_x + 2, 1, 1, 1), 0) + me_row * local_x - 1
    pos_y = lax.broadcasted_iota(jnp.int32, (1, local_y + 2, 1, 1), 1) + me_col * local_y - 1
    inside = (pos_x >= 0) & (pos_x < grid_x) & ((pos_y >= 0) & (pos_y < grid_y))
    middle = jnp.where(inside, middle, 0.0)
    return diffuse_margin(middle)


def solution(mesh):
    placed = (
        P("row", "col", None, None),
        P("row", "col", None, None),
        P("row", "col", None, None),
        P("row", "col"),
        P("row", None),
    )
    return jax.shard_map(
        body, mesh=mesh, in_specs=placed, out_specs=P("row", "col", None, None), check_vma=False
    )
```

```python
import functools

import jax
import jax.numpy as jnp
from jax import lax
from jax.experimental import pallas as pl
from jax.experimental.pallas import tpu as pltpu
from jax.sharding import PartitionSpec as P

diff_rate = 0.12
edge_scale = 0.5
BF16, F32 = jnp.bfloat16, jnp.float32


def swap(value, axis, distance):
    count = lax.axis_size(axis)
    return lax.ppermute(value, axis, [(i, i ^ distance) for i in range(count)])


def swap_odd(value, axis):
    count = lax.axis_size(axis)
    pairs = [(i, i + 1) for i in range(1, count - 1, 2)]
    return lax.ppermute(value, axis, pairs + [(b, a) for a, b in pairs])


def bits_of(count):
    bit, found = 1, []
    while bit < count:
        found.append(bit)
        bit *= 2
    return found


def dot_nt(a, b):
    return lax.dot_general(a, b, (((1,), (1,)), ((), ())), preferred_element_type=F32)


def call(kernel, name, scalars, arrays, outs, scratch=()):
    smem = pl.BlockSpec(memory_space=pltpu.SMEM)
    vmem = pl.BlockSpec(memory_space=pltpu.VMEM)
    return pl.pallas_call(
        kernel,
        name=name,
        out_shape=[jax.ShapeDtypeStruct(shape, kind) for shape, kind in outs],
        in_specs=[smem] * len(scalars) + [vmem] * len(arrays),
        out_specs=[vmem] * len(outs),
        scratch_shapes=list(scratch),
    )(*scalars, *arrays)


def cast_kernel(image_ref, out_ref):
    flat = image_ref[...].reshape(out_ref.shape[1], out_ref.shape[0])
    out_ref[...] = flat.T.astype(BF16)


def keep_rank(value, rank):
    level = lax.broadcasted_iota(jnp.int32, value.shape, 1)
    return jnp.where(level < rank, value, 0.0).astype(BF16)


def half_rows(u_ref, coef_ref, i, core):
    total = None
    for j in range(u_ref.shape[1]):
        rows = u_ref[i, j, :, core]
        rows = rows.reshape(rows.shape[0] * rows.shape[1], rows.shape[2])
        term = dot_nt(rows, coef_ref[i, j])
        total = term if total is None else total + term
    return total.reshape(u_ref.shape[2], u_ref.shape[4], total.shape[1])


def forward_kernel(count, at_ref, ranks_ref, *refs):
    pieces, (u_ref, v_ref, cross_ref, coef_ref, held) = refs[:count], refs[count:]
    row_tiles, col_tiles, chips = u_ref.shape[:3]
    me_row, me_col = at_ref[0], at_ref[1]
    for distance in range(count):
        held[me_row ^ distance] = pieces[distance][...]
    per_tile = count // col_tiles
    for j in range(col_tiles):
        lhs = jnp.concatenate([held[j * per_tile + p] for p in range(per_tile)], axis=1)
        for i in range(row_tiles):
            value = jnp.dot(lhs, v_ref[i, j], preferred_element_type=F32)
            coef_ref[i, j] = keep_rank(value, ranks_ref[i, j])
    chip, core = me_col // 2, me_col % 2
    for i in range(row_tiles):
        value = half_rows(u_ref, coef_ref, i, 1 - core)
        for q in range(chips):
            cross_ref[chip ^ q, i] = value[q].astype(cross_ref.dtype)


def own_kernel(at_ref, u_ref, coef_ref, mine_ref):
    me_col = at_ref[1]
    chip, core = me_col // 2, me_col % 2
    for i in range(u_ref.shape[0]):
        value = half_rows(u_ref, coef_ref, i, core)
        for q in range(u_ref.shape[2]):
            mine_ref[chip ^ q, i] = value[q]


def sum_kernel(at_ref, mine_ref, crossed_ref, measured_ref, own_ref, *send_refs):
    me_col = at_ref[1]
    value = mine_ref[0] + crossed_ref[0].astype(F32)
    own_ref[...] = value - measured_ref[:, me_col].astype(F32)
    for q, send_ref in enumerate(send_refs, 1):
        send_ref[...] = (mine_ref[q] + crossed_ref[q].astype(F32)).astype(BF16)


def resid_kernel(own_ref, *refs):
    out_ref = refs[-1]
    for i in range(own_ref.shape[0]):
        value = own_ref[i]
        for ref in refs[:-1]:
            value = value + ref[i].astype(F32)
        out_ref[i] = value.T.astype(BF16)


def gradient_piece(v_ref, back_ref, start, brick):
    tile_len = v_ref.shape[2]
    tile = start // tile_len
    inside = pl.multiple_of(start % tile_len, brick)
    total = None
    for i in range(v_ref.shape[0]):
        term = dot_nt(v_ref[i, tile, pl.ds(inside, brick)], back_ref[i, tile])
        total = term if total is None else total + term
    return total


def adjoint_kernel(count, at_ref, ranks_ref, *refs):
    pieces, (u_ref, v_ref, back_ref), rest = refs[:count], refs[count : count + 3], refs[count + 3 :]
    outs, held = rest[:-1], rest[-1]
    row_tiles, col_tiles = u_ref.shape[:2]
    me_row, me_col = at_ref[0], at_ref[1]
    for distance in range(count):
        held[me_col ^ distance] = pieces[distance][...]
    for i in range(row_tiles):
        lhs = jnp.concatenate([held[p, i] for p in range(count)], axis=1)
        for j in range(col_tiles):
            value = jnp.dot(lhs, u_ref[i, j], preferred_element_type=F32)
            back_ref[i, j] = keep_rank(value, ranks_ref[i, j])
    for n, out_ref in enumerate(outs):
        brick = out_ref.shape[0]
        out_ref[...] = gradient_piece(v_ref, back_ref, (me_row ^ (2 * n + 1)) * brick, brick).astype(BF16)


def adjoint_rest_kernel(at_ref, v_ref, back_ref, *outs):
    for n, out_ref in enumerate(outs):
        brick = out_ref.shape[0]
        out_ref[...] = gradient_piece(v_ref, back_ref, (at_ref[0] ^ (2 * n)) * brick, brick)


def move_kernel(count, at_ref, image_ref, part_ref, *refs):
    received, (moved_ref, even_ref, odd_ref, side_ref) = refs[:count], refs[count:]
    gradient = part_ref[...]
    for ref in received:
        gradient = gradient + ref[...].astype(F32)
    moved = image_ref[...] - gradient.reshape(image_ref.shape)
    moved_ref[...] = moved
    side_ref[...] = moved.astype(BF16)
    width = even_ref.shape[0]
    far = image_ref.shape[0] - width
    odd = at_ref[0] % 2
    even_ref[...] = moved_ref[pl.ds((1 - odd) * far, width)].astype(BF16)
    odd_ref[...] = moved_ref[pl.ds(odd * far, width)].astype(BF16)


def corner_kernel(at_ref, even_ref, odd_ref, to_even_ref, to_odd_ref):
    last = even_ref.shape[1] - 1
    row_odd, col_odd = at_ref[0] % 2, at_ref[1] % 2
    near, side = (1 - col_odd) * last, col_odd * last
    for out_ref, y in ((to_even_ref, near), (to_odd_ref, side)):
        low = jnp.where(row_odd == 1, even_ref[1, y], odd_ref[1, y])
        high = jnp.where(row_odd == 1, odd_ref[0, y], even_ref[0, y])
        out_ref[0] = low
        out_ref[1] = high


def flux(delta):
    scaled = delta / edge_scale
    return delta / (1.0 + scaled * scaled)


def diffuse_kernel(at_ref, moved_ref, row_even, row_odd, col_even, col_odd, corner_even, corner_odd, out_ref, field):
    nx, ny, depth, frames = moved_ref.shape
    rows, cols = at_ref[2], at_ref[3]
    me_row, me_col = at_ref[0], at_ref[1]
    r_odd, c_odd = me_row % 2, me_col % 2
    r_even, c_even = 1 - r_odd, 1 - c_odd
    field[2 : 2 + nx, 2 : 2 + ny] = moved_ref[...]
    far_x, far_y = nx + 2, ny + 2
    field[pl.ds(r_even * far_x, 2), 2 : 2 + ny] = row_even[...].astype(F32)
    field[pl.ds(r_odd * far_x, 2), 2 : 2 + ny] = row_odd[...].astype(F32)
    field[2 : 2 + nx, pl.ds(c_even * far_y, 2)] = col_even[...].astype(F32)
    field[2 : 2 + nx, pl.ds(c_odd * far_y, 2)] = col_odd[...].astype(F32)
    for y, ref in ((c_even * (ny + 1) + 1, corner_even), (c_odd * (ny + 1) + 1, corner_odd)):
        field[1, y] = ref[0].astype(F32)
        field[nx + 2, y] = ref[1].astype(F32)
    level = lax.broadcasted_iota(jnp.int32, (depth, frames), 0)
    low_x, high_x = me_row > 0, me_row < rows - 1
    low_y, high_y = me_col > 0, me_col < cols - 1

    def along_depth(u):
        below = jnp.where(level == 0, 0.0, pltpu.roll(u, 1, 0))
        down = flux(u - below)
        up = jnp.where(level == depth - 1, flux(-u), pltpu.roll(down, depth - 1, 0))
        return up - down

    def diffuse(cells, get):
        faces = {}

        def face(kind, x, y):
            key = (kind, x, y)
            if key not in faces:
                x2, y2 = (x + 1, y) if kind == 0 else (x, y + 1)
                faces[key] = flux(get(x2, y2) - get(x, y))
            return faces[key]

        new = {}
        for x, y in cells:
            u = get(x, y)
            total = face(0, x, y) - face(0, x - 1, y)
            total = total + (face(1, x, y) - face(1, x, y - 1))
            new[x, y] = u + diff_rate * (total + along_depth(u))
        return new

    inner = [(x, y) for x in range(2, 2 + nx) for y in range(2, 2 + ny)]
    ring = [(x, y) for x in (1, nx + 2) for y in range(2, 2 + ny)]
    ring += [(x, y) for x in range(2, 2 + nx) for y in (1, ny + 2)]
    first = diffuse(sorted(inner + ring), lambda x, y: field[x, y])
    for x, y in first:
        value = first[x, y]
        for at, end, open_end in ((x, 1, low_x), (x, nx + 2, high_x), (y, 1, low_y), (y, ny + 2, high_y)):
            if at == end:
                value = jnp.where(open_end, value, 0.0)
        field[x, y] = value
    second = diffuse(inner, lambda x, y: field[x, y])
    for x, y in inner:
        out_ref[x - 2, y - 2] = second[x, y]


def body(image, u_factors, v_factors, ranks, measured):
    row_tiles, col_tiles, tile_len, rank_max = u_factors.shape
    nx, ny, depth, frames = image.shape
    brick = nx * ny * depth
    rows, cols = lax.axis_size("row"), lax.axis_size("col")
    chips, part_len = cols // 2, tile_len // cols
    at = jnp.stack([lax.axis_index("row"), lax.axis_index("col"), rows, cols]).astype(jnp.int32)

    have = {0: call(cast_kernel, "cast", (), (image,), [((frames, brick), BF16)])[0]}
    for bit in reversed(bits_of(rows)):
        for distance in list(have):
            have[distance ^ bit] = swap(have[distance], "row", bit)
    pieces = [have[distance] for distance in range(rows)]

    u_parts = u_factors.reshape(row_tiles, col_tiles, chips, 2, part_len, rank_max)
    half = (chips, row_tiles, part_len, frames)
    cross, coef = call(
        functools.partial(forward_kernel, rows),
        "forward",
        (at, ranks),
        (*pieces, u_parts, v_factors),
        [(half, BF16), ((row_tiles, col_tiles, frames, rank_max), BF16)],
        [pltpu.VMEM((rows, frames, brick), BF16)],
    )
    crossed = swap(cross, "col", 1)
    (mine,) = call(own_kernel, "own", (at,), (u_parts, coef), [(half, F32)])
    part = (row_tiles, part_len, frames)
    own, *sends = call(
        sum_kernel,
        "sum",
        (at,),
        (mine, crossed, measured.reshape(row_tiles, cols, part_len, frames)),
        [(part, F32)] + [(part, BF16)] * (chips - 1),
    )
    received = [swap(value, "col", 2 * q) for q, value in enumerate(sends, 1)]
    (resid,) = call(
        resid_kernel, "resid", (), (own, *received), [((row_tiles, frames, part_len), BF16)]
    )
    parts = {}
    for q in range(chips):
        parts[2 * q] = swap(resid, "col", 2 * q) if q else resid
        parts[2 * q + 1] = swap(parts[2 * q], "col", 1)

    back, *odds = call(
        functools.partial(adjoint_kernel, cols),
        "adjoint",
        (at, ranks),
        (*[parts[d] for d in range(cols)], u_factors, v_factors),
        [((row_tiles, col_tiles, frames, rank_max), BF16)] + [((brick, frames), BF16)] * (rows // 2),
        [pltpu.VMEM((cols, row_tiles, frames, part_len), BF16)],
    )
    crossing = [swap(value, "row", 1) for value in odds]
    evens = call(
        adjoint_rest_kernel, "rest", (at,), (v_factors, back), [((brick, frames), F32)] * (rows // 2)
    )
    sums = {2 * n: (evens[n], [crossing[n]]) for n in range(rows // 2)}
    for bit in bits_of(rows)[1:]:
        for d in [d for d in sums if d & bit]:
            base, extra = sums.pop(d)
            for value in extra:
                base = base + value.astype(F32)
            sums[d ^ bit][1].append(swap(base.astype(BF16), "row", bit))
    base, extra = sums[0]

    edge = (2, ny, depth, frames)
    moved, to_even, to_odd, side = call(
        functools.partial(move_kernel, len(extra)),
        "move",
        (at,),
        (image, base, *extra),
        [(image.shape, F32), (edge, BF16), (edge, BF16), (image.shape, BF16)],
    )
    row_even, row_odd = swap(to_even, "row", 1), swap_odd(to_odd, "row")
    col_odd, col_even = swap_odd(side, "col"), swap(side, "col", 1)
    corner = (2, depth, frames)
    to_even, to_odd = call(
        corner_kernel, "corner", (at,), (row_even, row_odd), [(corner, BF16)] * 2
    )
    corner_odd, corner_even = swap_odd(to_odd, "col"), swap(to_even, "col", 1)
    return call(
        diffuse_kernel,
        "diffuse",
        (at,),
        (moved, row_even, row_odd, col_even, col_odd, corner_even, corner_odd),
        [(image.shape, F32)],
        [pltpu.VMEM((nx + 4, ny + 4, depth, frames), F32)],
    )[0]


def solution(mesh):
    placed = (
        P("row", "col", None, None),
        P("row", "col", None, None),
        P("row", "col", None, None),
        P("row", "col"),
        P("row", None),
    )
    return jax.shard_map(
        body, mesh=mesh, in_specs=placed, out_specs=P("row", "col", None, None), check_vma=False
    )
```

```python
import functools

import jax
import jax.numpy as jnp
from jax import lax
from jax.experimental import pallas as pl
from jax.experimental.pallas import tpu as pltpu
from jax.sharding import PartitionSpec as P


diff_rate = 0.12
edge_scale = 0.5
BF16, F32 = jnp.bfloat16, jnp.float32


def swap(value, axis, distance):
    count = lax.axis_size(axis)
    return lax.ppermute(value, axis, [(i, i ^ distance) for i in range(count)])


def swap_odd(value, axis):
    count = lax.axis_size(axis)
    pairs = [(i, i + 1) for i in range(1, count - 1, 2)]
    return lax.ppermute(value, axis, pairs + [(b, a) for a, b in pairs])


def bits_of(count):
    bit, found = 1, []
    while bit < count:
        found.append(bit)
        bit *= 2
    return found


def dot_nt(a, b):
    return lax.dot_general(a, b, (((1,), (1,)), ((), ())), preferred_element_type=F32)


def call(kernel, arrays, outs, scratch=(), kept=pltpu.VMEM, through=0):
    arrays = [pltpu.with_memory_space_constraint(value, pltpu.VMEM) for value in arrays]
    vmem = pl.BlockSpec(memory_space=pltpu.VMEM)
    count, made = len(arrays), len(outs)
    outs = [*outs, *[(value.shape, value.dtype) for value in arrays[count - through :]]]

    def run(*refs):
        kernel(*refs[: count + made], *refs[count + made + through :])

    return pl.pallas_call(
        run,
        out_shape=[kept(shape, kind) for shape, kind in outs],
        in_specs=[vmem] * count,
        out_specs=[vmem] * len(outs),
        input_output_aliases={count - through + n: made + n for n in range(through)},
        scratch_shapes=list(scratch),
        compiler_params=pltpu.CompilerParams(vmem_limit_bytes=2**23),
    )(*arrays)


def load_kernel(factor_ref, samples_ref, *refs):
    out_ref, wanted_ref, sems = refs[-3:]
    copies = [(factor_ref.at[i], out_ref.at[i]) for i in range(factor_ref.shape[0])]
    copies.append((samples_ref.at[:, lax.axis_index("col")], wanted_ref))
    copies = [pltpu.make_async_copy(a, b, sems.at[n]) for n, (a, b) in enumerate(copies)]
    for copy in copies:
        copy.start()
    for copy in copies:
        copy.wait()


def load(factors, samples, after):
    vmem, hbm = (pl.BlockSpec(memory_space=space) for space in (pltpu.VMEM, pltpu.HBM))
    parts = (samples.shape[0], *samples.shape[2:])
    return pl.pallas_call(
        load_kernel,
        out_shape=[pltpu.VMEM(factors.shape, factors.dtype), pltpu.VMEM(parts, samples.dtype)],
        in_specs=[hbm, hbm] + [vmem] * len(after),
        out_specs=[vmem, vmem],
        scratch_shapes=[pltpu.SemaphoreType.DMA((factors.shape[0] + 1,))],
        compiler_params=pltpu.CompilerParams(vmem_limit_bytes=2**23),
    )(
        *[pltpu.with_memory_space_constraint(value, pltpu.HBM) for value in (factors, samples)],
        *[pltpu.with_memory_space_constraint(value, pltpu.VMEM) for value in after],
    )


def cast_kernel(image_ref, out_ref):
    flat = image_ref[...].reshape(out_ref.shape[1], out_ref.shape[0])
    out_ref[...] = flat.T.astype(BF16)


def near_kernel(mask_ref, *refs):
    pieces, (v_ref, near_ref, held) = refs[:-3], refs[-3:]
    count, col_tiles = len(pieces), v_ref.shape[1]
    me_row = lax.axis_index("row")
    tile = me_row // count
    for distance in range(count):
        held[(me_row % count) ^ distance] = pieces[distance][...]
    lhs = jnp.concatenate([held[p] for p in range(count)], axis=1)
    for i in range(v_ref.shape[0]):
        value = jnp.dot(lhs, v_ref[i, tile], preferred_element_type=F32)
        near_ref[i] = (value * mask_ref[pl.ds(i * col_tiles + tile, 1)]).astype(BF16)


def half_rows(u_ref, coef_ref, i, core):
    total = None
    for j in range(u_ref.shape[1]):
        rows = u_ref[i, j, :, core]
        rows = rows.reshape(rows.shape[0] * rows.shape[1], rows.shape[2])
        term = dot_nt(rows, coef_ref[i, j])
        total = term if total is None else total + term
    return total.reshape(u_ref.shape[2], u_ref.shape[4], total.shape[1])


def forward_kernel(mask_ref, near_ref, *refs):
    pieces, (u_ref, v_ref, cross_ref, coef_ref, held) = refs[:-5], refs[-5:]
    row_tiles, col_tiles, chips = u_ref.shape[:3]
    per_tile = len(pieces) // (col_tiles - 1)
    me_row, me_col = lax.axis_index("row"), lax.axis_index("col")
    own_tile = me_row // per_tile
    for n, piece in enumerate(pieces, per_tile):
        held[me_row ^ n] = piece[...]
    for i in range(row_tiles):
        coef_ref[i, own_tile] = near_ref[i]
    for n in range(1, col_tiles):
        tile = own_tile ^ n
        lhs = jnp.concatenate([held[tile * per_tile + p] for p in range(per_tile)], axis=1)
        for i in range(row_tiles):
            value = jnp.dot(lhs, v_ref[i, tile], preferred_element_type=F32)
            coef_ref[i, tile] = (value * mask_ref[pl.ds(i * col_tiles + tile, 1)]).astype(BF16)
    chip, core = me_col // 2, me_col % 2
    for i in range(row_tiles):
        value = half_rows(u_ref, coef_ref, i, 1 - core)
        for q in range(chips):
            cross_ref[chip ^ q, i] = value[q].astype(cross_ref.dtype)


def own_kernel(coef_ref, u_ref, mine_ref):
    me_col = lax.axis_index("col")
    chip, core = me_col // 2, me_col % 2
    for i in range(u_ref.shape[0]):
        value = half_rows(u_ref, coef_ref, i, core)
        for q in range(u_ref.shape[2]):
            mine_ref[chip ^ q, i] = value[q]


def sum_kernel(mine_ref, crossed_ref, wanted_ref, own_ref, *send_refs):
    value = mine_ref[0] + crossed_ref[0].astype(F32)
    own_ref[...] = value - wanted_ref[...].astype(F32)
    for q, send_ref in enumerate(send_refs, 1):
        send_ref[...] = (mine_ref[q] + crossed_ref[q].astype(F32)).astype(BF16)


def resid_kernel(own_ref, *refs):
    out_ref = refs[-1]
    for i in range(own_ref.shape[0]):
        value = own_ref[i]
        for ref in refs[:-1]:
            value = value + ref[i].astype(F32)
        out_ref[i] = value.T.astype(BF16)


def back_tile(held, mask_ref, u_ref, tile, i):
    count, col_tiles = held.shape[0], u_ref.shape[1]
    lhs = jnp.concatenate([held[p, i] for p in range(count)], axis=1)
    value = jnp.dot(lhs, u_ref[i, tile], preferred_element_type=F32)
    return (value * mask_ref[pl.ds(i * col_tiles + tile, 1)]).astype(BF16)


def gradient_piece(v_ref, back_ref, tile, inside, brick):
    total = None
    for i in range(v_ref.shape[0]):
        term = dot_nt(v_ref[i, tile, pl.ds(inside, brick)], back_ref[i])
        total = term if total is None else total + term
    return total


def adjoint_kernel(count, first, mask_ref, *refs):
    pieces, (u_ref, v_ref), rest = refs[:count], refs[count : count + 2], refs[count + 2 :]
    outs, (held, back_ref) = rest[:-2], rest[-2:]
    row_tiles, tile_len = u_ref.shape[0], u_ref.shape[2]
    brick = outs[0].shape[0]
    per_tile = tile_len // brick
    me_row, me_col = lax.axis_index("row"), lax.axis_index("col")
    for distance in range(count):
        held[me_col ^ distance] = pieces[distance][...]
    for n in range(len(outs) // per_tile):
        tile = (me_row // per_tile) ^ (first + n)
        for i in range(row_tiles):
            back_ref[i] = back_tile(held, mask_ref, u_ref, tile, i)
        for p in reversed(range(per_tile)):
            inside = pl.multiple_of(((me_row % per_tile) ^ p) * brick, brick)
            out_ref = outs[n * per_tile + p]
            value = gradient_piece(v_ref, back_ref, tile, inside, brick)
            out_ref[...] = value.astype(out_ref.dtype)


def add_kernel(part_ref, *refs):
    value = part_ref[...]
    for ref in refs[:-1]:
        value = value + ref[...].astype(F32)
    refs[-1][...] = value.astype(BF16)


def move_kernel(image_ref, part_ref, *refs):
    received, (moved_ref, even_ref, odd_ref, side_ref) = refs[:-4], refs[-4:]
    gradient = part_ref[...]
    for ref in received:
        gradient = gradient + ref[...].astype(F32)
    moved = image_ref[...] - gradient.reshape(image_ref.shape)
    moved_ref[...] = moved
    side_ref[...] = moved.astype(BF16)
    width = even_ref.shape[0]
    far = image_ref.shape[0] - width
    odd = lax.axis_index("row") % 2
    even_ref[...] = moved_ref[pl.ds((1 - odd) * far, width)].astype(BF16)
    odd_ref[...] = moved_ref[pl.ds(odd * far, width)].astype(BF16)


def corner_kernel(even_ref, odd_ref, to_even_ref, to_odd_ref):
    last = even_ref.shape[1] - 1
    row_odd, col_odd = lax.axis_index("row") % 2, lax.axis_index("col") % 2
    near, side = (1 - col_odd) * last, col_odd * last
    for out_ref, y in ((to_even_ref, near), (to_odd_ref, side)):
        low = jnp.where(row_odd == 1, even_ref[1, y], odd_ref[1, y])
        high = jnp.where(row_odd == 1, odd_ref[0, y], even_ref[0, y])
        out_ref[0] = low
        out_ref[1] = high


def flux(delta):
    scaled = delta / edge_scale
    return delta / (1.0 + scaled * scaled)


def diffuse_kernel(moved_ref, row_even, row_odd, col_even, col_odd, corner_even, corner_odd, out_ref, field):
    nx, ny, depth, frames = moved_ref.shape
    rows, cols = lax.axis_size("row"), lax.axis_size("col")
    me_row, me_col = lax.axis_index("row"), lax.axis_index("col")
    r_odd, c_odd = me_row % 2, me_col % 2
    r_even, c_even = 1 - r_odd, 1 - c_odd
    field[2 : 2 + nx, 2 : 2 + ny] = moved_ref[...]
    far_x, far_y = nx + 2, ny + 2
    field[pl.ds(r_even * far_x, 2), 2 : 2 + ny] = row_even[...].astype(F32)
    field[pl.ds(r_odd * far_x, 2), 2 : 2 + ny] = row_odd[...].astype(F32)
    field[2 : 2 + nx, pl.ds(c_even * far_y, 2)] = col_even[...].astype(F32)
    field[2 : 2 + nx, pl.ds(c_odd * far_y, 2)] = col_odd[...].astype(F32)
    for y, ref in ((c_even * (ny + 1) + 1, corner_even), (c_odd * (ny + 1) + 1, corner_odd)):
        field[1, y] = ref[0].astype(F32)
        field[nx + 2, y] = ref[1].astype(F32)
    level = lax.broadcasted_iota(jnp.int32, (depth, frames), 0)
    low_x, high_x = me_row > 0, me_row < rows - 1
    low_y, high_y = me_col > 0, me_col < cols - 1

    def along_depth(u):
        below = jnp.where(level == 0, 0.0, pltpu.roll(u, 1, 0))
        down = flux(u - below)
        up = jnp.where(level == depth - 1, flux(-u), pltpu.roll(down, depth - 1, 0))
        return up - down

    def diffuse(cells, get):
        faces = {}

        def face(kind, x, y):
            key = (kind, x, y)
            if key not in faces:
                x2, y2 = (x + 1, y) if kind == 0 else (x, y + 1)
                faces[key] = flux(get(x2, y2) - get(x, y))
            return faces[key]

        new = {}
        for x, y in cells:
            u = get(x, y)
            total = face(0, x, y) - face(0, x - 1, y)
            total = total + (face(1, x, y) - face(1, x, y - 1))
            new[x, y] = u + diff_rate * (total + along_depth(u))
        return new

    inner = [(x, y) for x in range(2, 2 + nx) for y in range(2, 2 + ny)]
    ring = [(x, y) for x in (1, nx + 2) for y in range(2, 2 + ny)]
    ring += [(x, y) for x in range(2, 2 + nx) for y in (1, ny + 2)]
    first = diffuse(sorted(inner + ring), lambda x, y: field[x, y])
    for x, y in first:
        value = first[x, y]
        for at, end, open_end in ((x, 1, low_x), (x, nx + 2, high_x), (y, 1, low_y), (y, ny + 2, high_y)):
            if at == end:
                value = jnp.where(open_end, value, 0.0)
        field[x, y] = value
    second = diffuse(inner, lambda x, y: field[x, y])
    for x, y in inner:
        out_ref[x - 2, y - 2] = second[x, y]


def step(image, u_factors, v_factors, ranks, measured):
    row_tiles, col_tiles, tile_len, rank_max = u_factors.shape
    nx, ny, depth, frames = image.shape
    brick = nx * ny * depth
    per_tile = tile_len // brick
    rows, cols = lax.axis_size("row"), lax.axis_size("col")
    chips, part_len = cols // 2, tile_len // cols
    level = lax.broadcasted_iota(jnp.int32, (row_tiles * col_tiles, rank_max), 1)
    mask = (level < ranks.reshape(-1, 1)).astype(F32)
    samples = measured.reshape(row_tiles, cols, part_len, frames)

    own_x = call(cast_kernel, (image,), [((frames, brick), BF16)])[0]
    have = {0: own_x}
    for bit in reversed(bits_of(rows)):
        for distance in list(have):
            have[distance ^ bit] = swap(have[distance], "row", bit)
    pieces = [have[distance] for distance in range(rows)]
    v_factors, wanted = load(v_factors, samples, (own_x, mask))
    u_factors, _ = load(u_factors, samples, (own_x, mask))

    u_parts = u_factors.reshape(row_tiles, col_tiles, chips, 2, part_len, rank_max)
    half = (chips, row_tiles, part_len, frames)
    near, v_factors = call(
        near_kernel,
        (mask, *pieces[:per_tile], v_factors),
        [((row_tiles, frames, rank_max), BF16)],
        [pltpu.VMEM((per_tile, frames, brick), BF16)],
        through=1,
    )
    cross, coef, u_parts, v_factors = call(
        forward_kernel,
        (mask, near, *pieces[per_tile:], u_parts, v_factors),
        [(half, BF16), ((row_tiles, col_tiles, frames, rank_max), BF16)],
        [pltpu.VMEM((rows, frames, brick), BF16)],
        through=2,
    )
    crossed = swap(cross, "col", 1)
    mine, u_parts = call(own_kernel, (coef, u_parts), [(half, F32)], through=1)
    u_factors = u_parts.reshape(u_factors.shape)
    part = (row_tiles, part_len, frames)
    own, *sends = call(
        sum_kernel, (mine, crossed, wanted), [(part, F32)] + [(part, BF16)] * (chips - 1)
    )
    received = [swap(value, "col", 2 * q) for q, value in enumerate(sends, 1)]
    (resid,) = call(resid_kernel, (own, *received), [((row_tiles, frames, part_len), BF16)])
    parts = {}
    for q in range(chips):
        parts[2 * q] = swap(resid, "col", 2 * q) if q else resid
        parts[2 * q + 1] = swap(parts[2 * q], "col", 1)

    def adjoint(distances, kinds, u_factors, v_factors):
        return call(
            functools.partial(adjoint_kernel, cols, distances[0] // per_tile),
            (mask, *[parts[d] for d in range(cols)], u_factors, v_factors),
            [((brick, frames), kind) for kind in kinds],
            [
                pltpu.VMEM((cols, row_tiles, frames, part_len), BF16),
                pltpu.VMEM((row_tiles, frames, rank_max), BF16),
            ],
            through=2,
        )

    kinds = [BF16 if d % 2 else F32 for d in range(rows)]
    *far, u_factors, v_factors = adjoint(
        range(per_tile, rows), kinds[per_tile:], u_factors, v_factors
    )
    *close, u_factors, v_factors = adjoint(range(per_tile), kinds[:per_tile], u_factors, v_factors)
    terms = close + far
    sums = {}
    for d in range(0, rows, 2):
        sums[d] = (terms[d], [swap(terms[d + 1], "row", 1)])
    for bit in bits_of(rows)[1:]:
        for d in [d for d in sums if d & bit]:
            base, extra = sums.pop(d)
            (base,) = call(add_kernel, (base, *extra), [(base.shape, BF16)])
            sums[d ^ bit][1].append(swap(base, "row", bit))
    base, extra = sums[0]

    edge = (2, ny, depth, frames)
    moved, to_even, to_odd, side = call(
        move_kernel,
        (image, base, *extra),
        [(image.shape, F32), (edge, BF16), (edge, BF16), (image.shape, BF16)],
    )
    row_even = swap(to_even, "row", 1)
    row_odd = swap_odd(to_odd, "row")
    col_odd = swap_odd(side, "col")
    col_even = swap(side, "col", 1)
    corner = (2, depth, frames)
    to_even, to_odd = call(corner_kernel, (row_even, row_odd), [(corner, BF16)] * 2)
    corner_odd = swap_odd(to_odd, "col")
    corner_even = swap(to_even, "col", 1)
    return call(
        diffuse_kernel,
        (moved, row_even, row_odd, col_even, col_odd, corner_even, corner_odd),
        [(image.shape, F32)],
        [pltpu.VMEM((nx + 4, ny + 4, depth, frames), F32)],
        jax.ShapeDtypeStruct,
    )[0]


def solution(mesh):
    placed = (
        P("row", "col", None, None),
        P("row", "col", None, None),
        P("row", "col", None, None),
        P("row", "col"),
        P("row", None),
    )
    return jax.shard_map(
        step, mesh=mesh, in_specs=placed, out_specs=P("row", "col", None, None), check_vma=False
    )
```

```python
import functools

import jax
import jax.numpy as jnp
from jax import lax
from jax.experimental import pallas as pl
from jax.experimental.pallas import tpu as pltpu
from jax.sharding import PartitionSpec as P


diff_rate = 0.12
edge_scale = 0.5
BF16, F32 = jnp.bfloat16, jnp.float32


def swap(value, axis, distance):
    count = lax.axis_size(axis)
    return lax.ppermute(value, axis, [(i, i ^ distance) for i in range(count)])


def swap_odd(value, axis):
    rows, cols = lax.axis_size("row"), lax.axis_size("col")

    def partner(row, col):
        along, count = (row, rows) if axis == "row" else (col, cols)
        if along in (0, count - 1):
            return (row, col ^ 1) if axis == "row" else (row ^ 1, col)
        move = 1 if along % 2 else -1
        return (row + move, col) if axis == "row" else (row, col + move)

    pairs = []
    for row in range(rows):
        for col in range(cols):
            target = partner(row, col)
            pairs.append((row * cols + col, target[0] * cols + target[1]))
    return lax.ppermute(value, ("row", "col"), pairs)


def bits_of(count):
    bit, found = 1, []
    while bit < count:
        found.append(bit)
        bit *= 2
    return found


def dot_nt(a, b):
    return lax.dot_general(a, b, (((1,), (1,)), ((), ())), preferred_element_type=F32)


def call(kernel, arrays, outs, scratch=(), kept=pltpu.VMEM, through=0):
    arrays = [pltpu.with_memory_space_constraint(value, pltpu.VMEM) for value in arrays]
    vmem = pl.BlockSpec(memory_space=pltpu.VMEM)
    count, made = len(arrays), len(outs)
    outs = [*outs, *[(value.shape, value.dtype) for value in arrays[count - through :]]]

    def run(*refs):
        kernel(*refs[: count + made], *refs[count + made + through :])

    return pl.pallas_call(
        run,
        out_shape=[kept(shape, kind) for shape, kind in outs],
        in_specs=[vmem] * count,
        out_specs=[vmem] * len(outs),
        input_output_aliases={count - through + n: made + n for n in range(through)},
        scratch_shapes=list(scratch),
        compiler_params=pltpu.CompilerParams(vmem_limit_bytes=2**23),
    )(*arrays)


def load_kernel(factor_ref, samples_ref, *refs):
    out_ref, wanted_ref, sems = refs[-3:]
    copies = [(factor_ref.at[i], out_ref.at[i]) for i in range(factor_ref.shape[0])]
    copies.append((samples_ref.at[:, lax.axis_index("col")], wanted_ref))
    copies = [pltpu.make_async_copy(a, b, sems.at[n]) for n, (a, b) in enumerate(copies)]
    for copy in copies:
        copy.start()
    for copy in copies:
        copy.wait()


def load(factors, samples, after):
    vmem, hbm = (pl.BlockSpec(memory_space=space) for space in (pltpu.VMEM, pltpu.HBM))
    parts = (samples.shape[0], *samples.shape[2:])
    return pl.pallas_call(
        load_kernel,
        out_shape=[pltpu.VMEM(factors.shape, factors.dtype), pltpu.VMEM(parts, samples.dtype)],
        in_specs=[hbm, hbm] + [vmem] * len(after),
        out_specs=[vmem, vmem],
        scratch_shapes=[pltpu.SemaphoreType.DMA((factors.shape[0] + 1,))],
        compiler_params=pltpu.CompilerParams(vmem_limit_bytes=2**23),
    )(
        *[pltpu.with_memory_space_constraint(value, pltpu.HBM) for value in (factors, samples)],
        *[pltpu.with_memory_space_constraint(value, pltpu.VMEM) for value in after],
    )


def cast_kernel(image_ref, out_ref):
    flat = image_ref[...].reshape(out_ref.shape[1], out_ref.shape[0])
    out_ref[...] = flat.T.astype(BF16)


def near_kernel(mask_ref, *refs):
    pieces, (v_ref, near_ref, held) = refs[:-3], refs[-3:]
    count, col_tiles = len(pieces), v_ref.shape[1]
    me_row = lax.axis_index("row")
    tile = me_row // count
    for distance in range(count):
        held[(me_row % count) ^ distance] = pieces[distance][...]
    lhs = jnp.concatenate([held[p] for p in range(count)], axis=1)
    for i in range(v_ref.shape[0]):
        value = jnp.dot(lhs, v_ref[i, tile], preferred_element_type=F32)
        near_ref[i] = (value * mask_ref[pl.ds(i * col_tiles + tile, 1)]).astype(BF16)


def half_rows(u_ref, coef_ref, i, core):
    total = None
    for j in range(u_ref.shape[1]):
        rows = u_ref[i, j, :, core]
        rows = rows.reshape(rows.shape[0] * rows.shape[1], rows.shape[2])
        term = dot_nt(rows, coef_ref[i, j])
        total = term if total is None else total + term
    return total.reshape(u_ref.shape[2], u_ref.shape[4], total.shape[1])


def forward_kernel(mask_ref, near_ref, *refs):
    pieces, (u_ref, v_ref, cross_ref, coef_ref, held) = refs[:-5], refs[-5:]
    row_tiles, col_tiles, chips = u_ref.shape[:3]
    per_tile = len(pieces) // (col_tiles - 1)
    me_row, me_col = lax.axis_index("row"), lax.axis_index("col")
    own_tile = me_row // per_tile
    for n, piece in enumerate(pieces, per_tile):
        held[me_row ^ n] = piece[...]
    for i in range(row_tiles):
        coef_ref[i, own_tile] = near_ref[i]
    for n in range(1, col_tiles):
        tile = own_tile ^ n
        lhs = jnp.concatenate([held[tile * per_tile + p] for p in range(per_tile)], axis=1)
        for i in range(row_tiles):
            value = jnp.dot(lhs, v_ref[i, tile], preferred_element_type=F32)
            coef_ref[i, tile] = (value * mask_ref[pl.ds(i * col_tiles + tile, 1)]).astype(BF16)
    chip, core = me_col // 2, me_col % 2
    for i in range(row_tiles):
        value = half_rows(u_ref, coef_ref, i, 1 - core)
        for q in range(chips):
            cross_ref[chip ^ q, i] = value[q].astype(cross_ref.dtype)


def own_kernel(coef_ref, u_ref, mine_ref):
    me_col = lax.axis_index("col")
    chip, core = me_col // 2, me_col % 2
    for i in range(u_ref.shape[0]):
        value = half_rows(u_ref, coef_ref, i, core)
        for q in range(u_ref.shape[2]):
            mine_ref[chip ^ q, i] = value[q]


def sum_kernel(mine_ref, crossed_ref, wanted_ref, own_ref, *send_refs):
    value = mine_ref[0] + crossed_ref[0].astype(F32)
    own_ref[...] = value - wanted_ref[...].astype(F32)
    for q, send_ref in enumerate(send_refs, 1):
        send_ref[...] = (mine_ref[q] + crossed_ref[q].astype(F32)).astype(BF16)


def resid_kernel(own_ref, *refs):
    out_ref = refs[-1]
    for i in range(own_ref.shape[0]):
        value = own_ref[i]
        for ref in refs[:-1]:
            value = value + ref[i].astype(F32)
        out_ref[i] = value.T.astype(BF16)


def back_tile(held, mask_ref, u_ref, tile, i):
    count, col_tiles = held.shape[0], u_ref.shape[1]
    lhs = jnp.concatenate([held[p, i] for p in range(count)], axis=1)
    value = jnp.dot(lhs, u_ref[i, tile], preferred_element_type=F32)
    return (value * mask_ref[pl.ds(i * col_tiles + tile, 1)]).astype(BF16)


def gradient_piece(v_ref, back_ref, tile, inside, brick):
    total = None
    for i in range(v_ref.shape[0]):
        term = dot_nt(v_ref[i, tile, pl.ds(inside, brick)], back_ref[i])
        total = term if total is None else total + term
    return total


def adjoint_kernel(count, first, mask_ref, *refs):
    pieces, (u_ref, v_ref), rest = refs[:count], refs[count : count + 2], refs[count + 2 :]
    outs, (held, back_ref) = rest[:-2], rest[-2:]
    row_tiles, tile_len = u_ref.shape[0], u_ref.shape[2]
    brick = outs[0].shape[0]
    per_tile = tile_len // brick
    me_row, me_col = lax.axis_index("row"), lax.axis_index("col")
    for distance in range(count):
        held[me_col ^ distance] = pieces[distance][...]
    for n in range(len(outs) // per_tile):
        tile = (me_row // per_tile) ^ (first + n)
        for i in range(row_tiles):
            back_ref[i] = back_tile(held, mask_ref, u_ref, tile, i)
        for p in reversed(range(per_tile)):
            inside = pl.multiple_of(((me_row % per_tile) ^ p) * brick, brick)
            out_ref = outs[n * per_tile + p]
            value = gradient_piece(v_ref, back_ref, tile, inside, brick)
            out_ref[...] = value.astype(out_ref.dtype)


def add_kernel(part_ref, *refs):
    value = part_ref[...]
    for ref in refs[:-1]:
        value = value + ref[...].astype(F32)
    refs[-1][...] = value.astype(BF16)


def move_kernel(image_ref, part_ref, *refs):
    received, (moved_ref, even_ref, odd_ref, side_ref) = refs[:-4], refs[-4:]
    gradient = part_ref[...]
    for ref in received:
        gradient = gradient + ref[...].astype(F32)
    moved = image_ref[...] - gradient.reshape(image_ref.shape)
    moved_ref[...] = moved
    side_ref[...] = moved.astype(BF16)
    width = even_ref.shape[0]
    far = image_ref.shape[0] - width
    odd = lax.axis_index("row") % 2
    even_ref[...] = moved_ref[pl.ds((1 - odd) * far, width)].astype(BF16)
    odd_ref[...] = moved_ref[pl.ds(odd * far, width)].astype(BF16)


def corner_kernel(even_ref, odd_ref, to_even_ref, to_odd_ref):
    last = even_ref.shape[1] - 1
    row_odd, col_odd = lax.axis_index("row") % 2, lax.axis_index("col") % 2
    near, side = (1 - col_odd) * last, col_odd * last
    for out_ref, y in ((to_even_ref, near), (to_odd_ref, side)):
        low = jnp.where(row_odd == 1, even_ref[1, y], odd_ref[1, y])
        high = jnp.where(row_odd == 1, odd_ref[0, y], even_ref[0, y])
        out_ref[0] = low
        out_ref[1] = high


def flux(delta):
    scaled = delta / edge_scale
    return delta / (1.0 + scaled * scaled)


def diffuse_kernel(moved_ref, row_even, row_odd, col_even, col_odd, corner_even, corner_odd, out_ref, field):
    nx, ny, depth, frames = moved_ref.shape
    rows, cols = lax.axis_size("row"), lax.axis_size("col")
    me_row, me_col = lax.axis_index("row"), lax.axis_index("col")
    r_odd, c_odd = me_row % 2, me_col % 2
    r_even, c_even = 1 - r_odd, 1 - c_odd
    low_x, high_x = me_row > 0, me_row < rows - 1
    low_y, high_y = me_col > 0, me_col < cols - 1
    within = lambda ref, inside: jnp.where(inside, ref.astype(F32), 0.0)
    field[2 : 2 + nx, 2 : 2 + ny] = moved_ref[...]
    far_x, far_y = nx + 2, ny + 2
    field[pl.ds(r_even * far_x, 2), 2 : 2 + ny] = row_even[...].astype(F32)
    field[pl.ds(r_odd * far_x, 2), 2 : 2 + ny] = within(row_odd[...], low_x & high_x)
    field[2 : 2 + nx, pl.ds(c_even * far_y, 2)] = col_even[...].astype(F32)
    field[2 : 2 + nx, pl.ds(c_odd * far_y, 2)] = within(col_odd[...], low_y & high_y)
    for y, ref, inside in (
        (c_even * (ny + 1) + 1, corner_even, True),
        (c_odd * (ny + 1) + 1, corner_odd, low_y & high_y),
    ):
        field[1, y] = within(ref[0], low_x & inside)
        field[nx + 2, y] = within(ref[1], high_x & inside)
    level = lax.broadcasted_iota(jnp.int32, (depth, frames), 0)

    def along_depth(u):
        below = jnp.where(level == 0, 0.0, pltpu.roll(u, 1, 0))
        down = flux(u - below)
        up = jnp.where(level == depth - 1, flux(-u), pltpu.roll(down, depth - 1, 0))
        return up - down

    def diffuse(cells, get):
        faces = {}

        def face(kind, x, y):
            key = (kind, x, y)
            if key not in faces:
                x2, y2 = (x + 1, y) if kind == 0 else (x, y + 1)
                faces[key] = flux(get(x2, y2) - get(x, y))
            return faces[key]

        new = {}
        for x, y in cells:
            u = get(x, y)
            total = face(0, x, y) - face(0, x - 1, y)
            total = total + (face(1, x, y) - face(1, x, y - 1))
            new[x, y] = u + diff_rate * (total + along_depth(u))
        return new

    inner = [(x, y) for x in range(2, 2 + nx) for y in range(2, 2 + ny)]
    ring = [(x, y) for x in (1, nx + 2) for y in range(2, 2 + ny)]
    ring += [(x, y) for x in range(2, 2 + nx) for y in (1, ny + 2)]
    first = diffuse(sorted(inner + ring), lambda x, y: field[x, y])
    for x, y in first:
        value = first[x, y]
        for at, end, open_end in ((x, 1, low_x), (x, nx + 2, high_x), (y, 1, low_y), (y, ny + 2, high_y)):
            if at == end:
                value = jnp.where(open_end, value, 0.0)
        field[x, y] = value
    second = diffuse(inner, lambda x, y: field[x, y])
    for x, y in inner:
        out_ref[x - 2, y - 2] = second[x, y]


def step(image, u_factors, v_factors, ranks, measured):
    row_tiles, col_tiles, tile_len, rank_max = u_factors.shape
    nx, ny, depth, frames = image.shape
    brick = nx * ny * depth
    per_tile = tile_len // brick
    rows, cols = lax.axis_size("row"), lax.axis_size("col")
    chips, part_len = cols // 2, tile_len // cols
    level = lax.broadcasted_iota(jnp.int32, (row_tiles * col_tiles, rank_max), 1)
    mask = (level < ranks.reshape(-1, 1)).astype(F32)
    samples = measured.reshape(row_tiles, cols, part_len, frames)

    own_x = call(cast_kernel, (image,), [((frames, brick), BF16)])[0]
    have = {0: own_x}
    for bit in reversed(bits_of(rows)):
        for distance in list(have):
            have[distance ^ bit] = swap(have[distance], "row", bit)
    pieces = [have[distance] for distance in range(rows)]
    v_factors, wanted = load(v_factors, samples, (own_x, mask))
    u_factors, _ = load(u_factors, samples, (own_x, mask))

    u_parts = u_factors.reshape(row_tiles, col_tiles, chips, 2, part_len, rank_max)
    half = (chips, row_tiles, part_len, frames)
    near, v_factors = call(
        near_kernel,
        (mask, *pieces[:per_tile], v_factors),
        [((row_tiles, frames, rank_max), BF16)],
        [pltpu.VMEM((per_tile, frames, brick), BF16)],
        through=1,
    )
    cross, coef, u_parts, v_factors = call(
        forward_kernel,
        (mask, near, *pieces[per_tile:], u_parts, v_factors),
        [(half, BF16), ((row_tiles, col_tiles, frames, rank_max), BF16)],
        [pltpu.VMEM((rows, frames, brick), BF16)],
        through=2,
    )
    crossed = swap(cross, "col", 1)
    mine, u_parts = call(own_kernel, (coef, u_parts), [(half, F32)], through=1)
    u_factors = u_parts.reshape(u_factors.shape)
    part = (row_tiles, part_len, frames)
    own, *sends = call(
        sum_kernel, (mine, crossed, wanted), [(part, F32)] + [(part, BF16)] * (chips - 1)
    )
    received = [swap(value, "col", 2 * q) for q, value in enumerate(sends, 1)]
    (resid,) = call(resid_kernel, (own, *received), [((row_tiles, frames, part_len), BF16)])
    parts = {}
    for q in range(chips):
        parts[2 * q] = swap(resid, "col", 2 * q) if q else resid
        parts[2 * q + 1] = swap(parts[2 * q], "col", 1)

    def adjoint(distances, kinds, u_factors, v_factors):
        return call(
            functools.partial(adjoint_kernel, cols, distances[0] // per_tile),
            (mask, *[parts[d] for d in range(cols)], u_factors, v_factors),
            [((brick, frames), kind) for kind in kinds],
            [
                pltpu.VMEM((cols, row_tiles, frames, part_len), BF16),
                pltpu.VMEM((row_tiles, frames, rank_max), BF16),
            ],
            through=2,
        )

    kinds = [BF16 if d % 2 else F32 for d in range(rows)]
    *far, u_factors, v_factors = adjoint(
        range(per_tile, rows), kinds[per_tile:], u_factors, v_factors
    )
    *close, u_factors, v_factors = adjoint(range(per_tile), kinds[:per_tile], u_factors, v_factors)
    terms = close + far
    sums = {}
    for d in range(0, rows, 2):
        sums[d] = (terms[d], [swap(terms[d + 1], "row", 1)])
    for bit in bits_of(rows)[1:]:
        for d in [d for d in sums if d & bit]:
            base, extra = sums.pop(d)
            (base,) = call(add_kernel, (base, *extra), [(base.shape, BF16)])
            sums[d ^ bit][1].append(swap(base, "row", bit))
    base, extra = sums[0]

    edge = (2, ny, depth, frames)
    moved, to_even, to_odd, side = call(
        move_kernel,
        (image, base, *extra),
        [(image.shape, F32), (edge, BF16), (edge, BF16), (image.shape, BF16)],
    )
    row_even = swap(to_even, "row", 1)
    row_odd = swap_odd(to_odd, "row")
    col_odd = swap_odd(side, "col")
    col_even = swap(side, "col", 1)
    corner = (2, depth, frames)
    to_even, to_odd = call(corner_kernel, (row_even, row_odd), [(corner, BF16)] * 2)
    corner_odd = swap_odd(to_odd, "col")
    corner_even = swap(to_even, "col", 1)
    return call(
        diffuse_kernel,
        (moved, row_even, row_odd, col_even, col_odd, corner_even, corner_odd),
        [(image.shape, F32)],
        [pltpu.VMEM((nx + 4, ny + 4, depth, frames), F32)],
        jax.ShapeDtypeStruct,
    )[0]


def solution(mesh):
    placed = (
        P("row", "col", None, None),
        P("row", "col", None, None),
        P("row", "col", None, None),
        P("row", "col"),
        P("row", None),
    )
    return jax.shard_map(
        step, mesh=mesh, in_specs=placed, out_specs=P("row", "col", None, None), check_vma=False
    )
```

```python
import functools

import jax
import jax.numpy as jnp
from jax import lax
from jax.experimental import pallas as pl
from jax.experimental.pallas import tpu as pltpu
from jax.sharding import PartitionSpec as P


diff_rate = 0.12
edge_scale = 0.5
BF16, F32 = jnp.bfloat16, jnp.float32


def swap(value, axis, distance):
    count = lax.axis_size(axis)
    return lax.ppermute(value, axis, [(i, i ^ distance) for i in range(count)])


def swap_odd(value, axis):
    rows, cols = lax.axis_size("row"), lax.axis_size("col")

    def partner(row, col):
        along, count = (row, rows) if axis == "row" else (col, cols)
        if along in (0, count - 1):
            return (row, col ^ 1) if axis == "row" else (row ^ 1, col)
        move = 1 if along % 2 else -1
        return (row + move, col) if axis == "row" else (row, col + move)

    pairs = []
    for row in range(rows):
        for col in range(cols):
            target = partner(row, col)
            pairs.append((row * cols + col, target[0] * cols + target[1]))
    return lax.ppermute(value, ("row", "col"), pairs)


def bits_of(count):
    bit, found = 1, []
    while bit < count:
        found.append(bit)
        bit *= 2
    return found


def dot_nt(a, b):
    return lax.dot_general(a, b, (((1,), (1,)), ((), ())), preferred_element_type=F32)


def call(kernel, arrays, outs, scratch=(), kept=pltpu.VMEM, through=0):
    arrays = [pltpu.with_memory_space_constraint(value, pltpu.VMEM) for value in arrays]
    vmem = pl.BlockSpec(memory_space=pltpu.VMEM)
    count, made = len(arrays), len(outs)
    outs = [*outs, *[(value.shape, value.dtype) for value in arrays[count - through :]]]

    def run(*refs):
        kernel(*refs[: count + made], *refs[count + made + through :])

    return pl.pallas_call(
        run,
        out_shape=[kept(shape, kind) for shape, kind in outs],
        in_specs=[vmem] * count,
        out_specs=[vmem] * len(outs),
        input_output_aliases={count - through + n: made + n for n in range(through)},
        scratch_shapes=list(scratch),
        compiler_params=pltpu.CompilerParams(vmem_limit_bytes=2**23),
    )(*arrays)


def load_kernel(factor_ref, samples_ref, *refs):
    out_ref, wanted_ref, sems = refs[-3:]
    copies = [(factor_ref.at[i], out_ref.at[i]) for i in range(factor_ref.shape[0])]
    copies.append((samples_ref.at[:, lax.axis_index("col")], wanted_ref))
    copies = [pltpu.make_async_copy(a, b, sems.at[n]) for n, (a, b) in enumerate(copies)]
    for copy in copies:
        copy.start()
    for copy in copies:
        copy.wait()


def load(factors, samples, after):
    vmem, hbm = (pl.BlockSpec(memory_space=space) for space in (pltpu.VMEM, pltpu.HBM))
    parts = (samples.shape[0], *samples.shape[2:])
    return pl.pallas_call(
        load_kernel,
        out_shape=[pltpu.VMEM(factors.shape, factors.dtype), pltpu.VMEM(parts, samples.dtype)],
        in_specs=[hbm, hbm] + [vmem] * len(after),
        out_specs=[vmem, vmem],
        scratch_shapes=[pltpu.SemaphoreType.DMA((factors.shape[0] + 1,))],
        compiler_params=pltpu.CompilerParams(vmem_limit_bytes=2**23),
    )(
        *[pltpu.with_memory_space_constraint(value, pltpu.HBM) for value in (factors, samples)],
        *[pltpu.with_memory_space_constraint(value, pltpu.VMEM) for value in after],
    )


def cast_kernel(image_ref, out_ref):
    flat = image_ref[...].reshape(out_ref.shape[1], out_ref.shape[0])
    out_ref[...] = flat.T.astype(BF16)


def near_kernel(mask_ref, *refs):
    pieces, (v_ref, near_ref, held) = refs[:-3], refs[-3:]
    count, col_tiles = len(pieces), v_ref.shape[1]
    me_row = lax.axis_index("row")
    tile = me_row // count
    for distance in range(count):
        held[(me_row % count) ^ distance] = pieces[distance][...]
    lhs = jnp.concatenate([held[p] for p in range(count)], axis=1)
    for i in range(v_ref.shape[0]):
        value = jnp.dot(lhs, v_ref[i, tile], preferred_element_type=F32)
        near_ref[i] = (value * mask_ref[pl.ds(i * col_tiles + tile, 1)]).astype(BF16)


def half_rows(u_ref, coef_ref, i, low, core):
    total = None
    for j in range(u_ref.shape[1]):
        rows = u_ref[low + i, j, :, core]
        rows = rows.reshape(rows.shape[0] * rows.shape[1], rows.shape[2])
        term = dot_nt(rows, coef_ref[i, j])
        total = term if total is None else total + term
    return total.reshape(u_ref.shape[2], u_ref.shape[4], total.shape[1])


def forward_kernel(low, mask_ref, near_ref, *refs):
    pieces, (u_ref, v_ref, cross_ref, coef_ref, held) = refs[:-5], refs[-5:]
    col_tiles, chips = u_ref.shape[1:3]
    per_tile = len(pieces) // (col_tiles - 1)
    me_row, me_col = lax.axis_index("row"), lax.axis_index("col")
    own_tile = me_row // per_tile
    for n, piece in enumerate(pieces, per_tile):
        held[me_row ^ n] = piece[...]
    for i in range(coef_ref.shape[0]):
        coef_ref[i, own_tile] = near_ref[low + i]
    for n in range(1, col_tiles):
        tile = own_tile ^ n
        lhs = jnp.concatenate([held[tile * per_tile + p] for p in range(per_tile)], axis=1)
        for i in range(coef_ref.shape[0]):
            value = jnp.dot(lhs, v_ref[low + i, tile], preferred_element_type=F32)
            value = value * mask_ref[pl.ds((low + i) * col_tiles + tile, 1)]
            coef_ref[i, tile] = value.astype(BF16)
    chip, core = me_col // 2, me_col % 2
    for i in range(coef_ref.shape[0]):
        value = half_rows(u_ref, coef_ref, i, low, 1 - core)
        for q in range(chips):
            cross_ref[chip ^ q, i] = value[q].astype(cross_ref.dtype)


def own_kernel(low, coef_ref, u_ref, mine_ref):
    me_col = lax.axis_index("col")
    chip, core = me_col // 2, me_col % 2
    for i in range(coef_ref.shape[0]):
        value = half_rows(u_ref, coef_ref, i, low, core)
        for q in range(u_ref.shape[2]):
            mine_ref[chip ^ q, i] = value[q]


def sum_kernel(low, mine_ref, crossed_ref, wanted_ref, own_ref, *send_refs):
    value = mine_ref[0] + crossed_ref[0].astype(F32)
    own_ref[...] = value - wanted_ref[pl.ds(low, own_ref.shape[0])].astype(F32)
    for q, send_ref in enumerate(send_refs, 1):
        send_ref[...] = (mine_ref[q] + crossed_ref[q].astype(F32)).astype(BF16)


def resid_kernel(own_ref, *refs):
    out_ref = refs[-1]
    for i in range(own_ref.shape[0]):
        value = own_ref[i]
        for ref in refs[:-1]:
            value = value + ref[i].astype(F32)
        out_ref[i] = value.T.astype(BF16)


def hold(held, pieces):
    me_col = lax.axis_index("col")
    for distance, piece in enumerate(pieces):
        held[me_col ^ distance] = piece[...]


def back_tile(held, mask_ref, u_ref, tile, i, low):
    count, col_tiles = held.shape[0], u_ref.shape[1]
    lhs = jnp.concatenate([held[p, i] for p in range(count)], axis=1)
    value = jnp.dot(lhs, u_ref[low + i, tile], preferred_element_type=F32)
    return (value * mask_ref[pl.ds((low + i) * col_tiles + tile, 1)]).astype(BF16)


def back_kernel(mask_ref, *refs):
    pieces, (u_ref, back_ref, held) = refs[:-3], refs[-3:]
    hold(held, pieces)
    for i in range(back_ref.shape[0]):
        for tile in range(u_ref.shape[1]):
            back_ref[i, tile] = back_tile(held, mask_ref, u_ref, tile, i, 0)


def adjoint_kernel(count, first, mask_ref, early_ref, *refs):
    pieces, (u_ref, v_ref), rest = refs[:count], refs[count : count + 2], refs[count + 2 :]
    outs, (held, back_ref) = rest[:-2], rest[-2:]
    row_tiles, tile_len = u_ref.shape[0], u_ref.shape[2]
    low = early_ref.shape[0]
    brick = outs[0].shape[0]
    per_tile = tile_len // brick
    me_row = lax.axis_index("row")
    hold(held, pieces)
    for n in range(len(outs) // per_tile):
        tile = (me_row // per_tile) ^ (first + n)
        for i in range(row_tiles - low):
            back_ref[i] = back_tile(held, mask_ref, u_ref, tile, i, low)
        for p in reversed(range(per_tile)):
            inside = pl.multiple_of(((me_row % per_tile) ^ p) * brick, brick)
            value = None
            for i in range(row_tiles):
                back = early_ref[i, tile] if i < low else back_ref[i - low]
                term = dot_nt(v_ref[i, tile, pl.ds(inside, brick)], back)
                value = term if value is None else value + term
            out_ref = outs[n * per_tile + p]
            out_ref[...] = value.astype(out_ref.dtype)


def add_kernel(part_ref, *refs):
    value = part_ref[...]
    for ref in refs[:-1]:
        value = value + ref[...].astype(F32)
    refs[-1][...] = value.astype(BF16)


def move_kernel(image_ref, part_ref, *refs):
    received, (moved_ref, even_ref, odd_ref, side_ref) = refs[:-4], refs[-4:]
    gradient = part_ref[...]
    for ref in received:
        gradient = gradient + ref[...].astype(F32)
    moved = image_ref[...] - gradient.reshape(image_ref.shape)
    moved_ref[...] = moved
    side_ref[...] = moved.astype(BF16)
    width = even_ref.shape[0]
    far = image_ref.shape[0] - width
    odd = lax.axis_index("row") % 2
    even_ref[...] = moved_ref[pl.ds((1 - odd) * far, width)].astype(BF16)
    odd_ref[...] = moved_ref[pl.ds(odd * far, width)].astype(BF16)


def corner_kernel(even_ref, odd_ref, to_even_ref, to_odd_ref):
    last = even_ref.shape[1] - 1
    row_odd, col_odd = lax.axis_index("row") % 2, lax.axis_index("col") % 2
    near, side = (1 - col_odd) * last, col_odd * last
    for out_ref, y in ((to_even_ref, near), (to_odd_ref, side)):
        low = jnp.where(row_odd == 1, even_ref[1, y], odd_ref[1, y])
        high = jnp.where(row_odd == 1, odd_ref[0, y], even_ref[0, y])
        out_ref[0] = low
        out_ref[1] = high


def flux(delta):
    scaled = delta / edge_scale
    return delta / (1.0 + scaled * scaled)


def diffuse_kernel(moved_ref, row_even, row_odd, col_even, col_odd, corner_even, corner_odd, out_ref, field):
    nx, ny, depth, frames = moved_ref.shape
    rows, cols = lax.axis_size("row"), lax.axis_size("col")
    me_row, me_col = lax.axis_index("row"), lax.axis_index("col")
    r_odd, c_odd = me_row % 2, me_col % 2
    r_even, c_even = 1 - r_odd, 1 - c_odd
    low_x, high_x = me_row > 0, me_row < rows - 1
    low_y, high_y = me_col > 0, me_col < cols - 1
    within = lambda ref, inside: jnp.where(inside, ref.astype(F32), 0.0)
    field[2 : 2 + nx, 2 : 2 + ny] = moved_ref[...]
    far_x, far_y = nx + 2, ny + 2
    field[pl.ds(r_even * far_x, 2), 2 : 2 + ny] = row_even[...].astype(F32)
    field[pl.ds(r_odd * far_x, 2), 2 : 2 + ny] = within(row_odd[...], low_x & high_x)
    field[2 : 2 + nx, pl.ds(c_even * far_y, 2)] = col_even[...].astype(F32)
    field[2 : 2 + nx, pl.ds(c_odd * far_y, 2)] = within(col_odd[...], low_y & high_y)
    for y, ref, inside in (
        (c_even * (ny + 1) + 1, corner_even, True),
        (c_odd * (ny + 1) + 1, corner_odd, low_y & high_y),
    ):
        field[1, y] = within(ref[0], low_x & inside)
        field[nx + 2, y] = within(ref[1], high_x & inside)
    level = lax.broadcasted_iota(jnp.int32, (depth, frames), 0)

    def along_depth(u):
        below = jnp.where(level == 0, 0.0, pltpu.roll(u, 1, 0))
        down = flux(u - below)
        up = jnp.where(level == depth - 1, flux(-u), pltpu.roll(down, depth - 1, 0))
        return up - down

    def diffuse(cells, get):
        faces = {}

        def face(kind, x, y):
            key = (kind, x, y)
            if key not in faces:
                x2, y2 = (x + 1, y) if kind == 0 else (x, y + 1)
                faces[key] = flux(get(x2, y2) - get(x, y))
            return faces[key]

        new = {}
        for x, y in cells:
            u = get(x, y)
            total = face(0, x, y) - face(0, x - 1, y)
            total = total + (face(1, x, y) - face(1, x, y - 1))
            new[x, y] = u + diff_rate * (total + along_depth(u))
        return new

    inner = [(x, y) for x in range(2, 2 + nx) for y in range(2, 2 + ny)]
    ring = [(x, y) for x in (1, nx + 2) for y in range(2, 2 + ny)]
    ring += [(x, y) for x in range(2, 2 + nx) for y in (1, ny + 2)]
    first = diffuse(sorted(inner + ring), lambda x, y: field[x, y])
    for x, y in first:
        value = first[x, y]
        for at, end, open_end in ((x, 1, low_x), (x, nx + 2, high_x), (y, 1, low_y), (y, ny + 2, high_y)):
            if at == end:
                value = jnp.where(open_end, value, 0.0)
        field[x, y] = value
    second = diffuse(inner, lambda x, y: field[x, y])
    for x, y in inner:
        out_ref[x - 2, y - 2] = second[x, y]


def step(image, u_factors, v_factors, ranks, measured):
    row_tiles, col_tiles, tile_len, rank_max = u_factors.shape
    nx, ny, depth, frames = image.shape
    brick = nx * ny * depth
    per_tile = tile_len // brick
    rows, cols = lax.axis_size("row"), lax.axis_size("col")
    chips, part_len = cols // 2, tile_len // cols
    level = lax.broadcasted_iota(jnp.int32, (row_tiles * col_tiles, rank_max), 1)
    mask = (level < ranks.reshape(-1, 1)).astype(F32)
    samples = measured.reshape(row_tiles, cols, part_len, frames)

    own_x = call(cast_kernel, (image,), [((frames, brick), BF16)])[0]
    have = {0: own_x}
    for bit in reversed(bits_of(rows)):
        for distance in list(have):
            have[distance ^ bit] = swap(have[distance], "row", bit)
    pieces = [have[distance] for distance in range(rows)]
    v_factors, wanted = load(v_factors, samples, (own_x, mask))
    u_factors, _ = load(u_factors, samples, (own_x, mask))

    u_factors = u_factors.reshape(row_tiles, col_tiles, chips, 2, part_len, rank_max)
    split = (row_tiles + 1) // 2
    groups = [(0, split), (split, row_tiles - split)]
    near, v_factors = call(
        near_kernel,
        (mask, *pieces[:per_tile], v_factors),
        [((row_tiles, frames, rank_max), BF16)],
        [pltpu.VMEM((per_tile, frames, brick), BF16)],
        through=1,
    )
    crossed, mine = [], []
    for low, size in groups:
        half = (chips, size, part_len, frames)
        cross, coef, u_factors, v_factors = call(
            functools.partial(forward_kernel, low),
            (mask, near, *pieces[per_tile:], u_factors, v_factors),
            [(half, BF16), ((size, col_tiles, frames, rank_max), BF16)],
            [pltpu.VMEM((rows, frames, brick), BF16)],
            through=2,
        )
        crossed.append(swap(cross, "col", 1))
        value, u_factors = call(
            functools.partial(own_kernel, low), (coef, u_factors), [(half, F32)], through=1
        )
        mine.append(value)
    u_factors = u_factors.reshape(row_tiles, col_tiles, tile_len, rank_max)
    own, received = [], []
    for n, (low, size) in enumerate(groups):
        part = (size, part_len, frames)
        value, *sends = call(
            functools.partial(sum_kernel, low),
            (mine[n], crossed[n], wanted),
            [(part, F32)] + [(part, BF16)] * (chips - 1),
        )
        own.append(value)
        received.append([])
        for q, value in enumerate(sends, 1):
            received[n].append(swap(value, "col", 2 * q))
    parts = []
    for n, (low, size) in enumerate(groups):
        (resid,) = call(resid_kernel, (own[n], *received[n]), [((size, frames, part_len), BF16)])
        pieces = {}
        for q in range(chips):
            pieces[2 * q] = swap(resid, "col", 2 * q) if q else resid
            pieces[2 * q + 1] = swap(pieces[2 * q], "col", 1)
        parts.append([pieces[d] for d in range(cols)])
    size = groups[0][1]
    early, u_factors = call(
        back_kernel,
        (mask, *parts[0], u_factors),
        [((size, col_tiles, frames, rank_max), BF16)],
        [pltpu.VMEM((cols, size, frames, part_len), BF16)],
        through=1,
    )

    def adjoint(distances, kinds, u_factors, v_factors):
        size = groups[1][1]
        return call(
            functools.partial(adjoint_kernel, cols, distances[0] // per_tile),
            (mask, early, *parts[1], u_factors, v_factors),
            [((brick, frames), kind) for kind in kinds],
            [
                pltpu.VMEM((cols, size, frames, part_len), BF16),
                pltpu.VMEM((size, frames, rank_max), BF16),
            ],
            through=2,
        )

    kinds = [BF16 if d % 2 else F32 for d in range(rows)]
    *far, u_factors, v_factors = adjoint(
        range(per_tile, rows), kinds[per_tile:], u_factors, v_factors
    )
    *close, u_factors, v_factors = adjoint(range(per_tile), kinds[:per_tile], u_factors, v_factors)
    terms = close + far
    sums = {}
    for d in range(0, rows, 2):
        sums[d] = (terms[d], [swap(terms[d + 1], "row", 1)])
    for bit in bits_of(rows)[1:]:
        for d in [d for d in sums if d & bit]:
            base, extra = sums.pop(d)
            (base,) = call(add_kernel, (base, *extra), [(base.shape, BF16)])
            sums[d ^ bit][1].append(swap(base, "row", bit))
    base, extra = sums[0]

    edge = (2, ny, depth, frames)
    moved, to_even, to_odd, side = call(
        move_kernel,
        (image, base, *extra),
        [(image.shape, F32), (edge, BF16), (edge, BF16), (image.shape, BF16)],
    )
    row_even = swap(to_even, "row", 1)
    row_odd = swap_odd(to_odd, "row")
    col_odd = swap_odd(side, "col")
    col_even = swap(side, "col", 1)
    corner = (2, depth, frames)
    to_even, to_odd = call(corner_kernel, (row_even, row_odd), [(corner, BF16)] * 2)
    corner_odd = swap_odd(to_odd, "col")
    corner_even = swap(to_even, "col", 1)
    return call(
        diffuse_kernel,
        (moved, row_even, row_odd, col_even, col_odd, corner_even, corner_odd),
        [(image.shape, F32)],
        [pltpu.VMEM((nx + 4, ny + 4, depth, frames), F32)],
        jax.ShapeDtypeStruct,
    )[0]


def solution(mesh):
    placed = (
        P("row", "col", None, None),
        P("row", "col", None, None),
        P("row", "col", None, None),
        P("row", "col"),
        P("row", None),
    )
    return jax.shard_map(
        step, mesh=mesh, in_specs=placed, out_specs=P("row", "col", None, None), check_vma=False
    )
```

```python
import functools

import jax
import jax.numpy as jnp
from jax import lax
from jax.experimental import pallas as pl
from jax.experimental.pallas import tpu as pltpu
from jax.sharding import PartitionSpec as P


diff_rate = 0.12
edge_scale = 0.5
BF16, F32 = jnp.bfloat16, jnp.float32


def swap(value, axis, distance):
    count = lax.axis_size(axis)
    return lax.ppermute(value, axis, [(i, i ^ distance) for i in range(count)])


def swap_odd(value, axis):
    rows, cols = lax.axis_size("row"), lax.axis_size("col")

    def partner(row, col):
        along, count = (row, rows) if axis == "row" else (col, cols)
        if along in (0, count - 1):
            return (row, col ^ 1) if axis == "row" else (row ^ 1, col)
        move = 1 if along % 2 else -1
        return (row + move, col) if axis == "row" else (row, col + move)

    pairs = []
    for row in range(rows):
        for col in range(cols):
            target = partner(row, col)
            pairs.append((row * cols + col, target[0] * cols + target[1]))
    return lax.ppermute(value, ("row", "col"), pairs)


def bits_of(count):
    bit, found = 1, []
    while bit < count:
        found.append(bit)
        bit *= 2
    return found


def dot_nt(a, b):
    return lax.dot_general(a, b, (((1,), (1,)), ((), ())), preferred_element_type=F32)


def call(kernel, arrays, outs, scratch=(), kept=pltpu.VMEM, through=0):
    arrays = [pltpu.with_memory_space_constraint(value, pltpu.VMEM) for value in arrays]
    vmem = pl.BlockSpec(memory_space=pltpu.VMEM)
    count, made = len(arrays), len(outs)
    outs = [*outs, *[(value.shape, value.dtype) for value in arrays[count - through :]]]

    def run(*refs):
        kernel(*refs[: count + made], *refs[count + made + through :])

    return pl.pallas_call(
        run,
        out_shape=[kept(shape, kind) for shape, kind in outs],
        in_specs=[vmem] * count,
        out_specs=[vmem] * len(outs),
        input_output_aliases={count - through + n: made + n for n in range(through)},
        scratch_shapes=list(scratch),
        compiler_params=pltpu.CompilerParams(vmem_limit_bytes=2**23),
    )(*arrays)


def load_kernel(factor_ref, samples_ref, *refs):
    out_ref, wanted_ref, sems = refs[-3:]
    copies = [(factor_ref.at[i], out_ref.at[i]) for i in range(factor_ref.shape[0])]
    copies.append((samples_ref.at[:, lax.axis_index("col")], wanted_ref))
    copies = [pltpu.make_async_copy(a, b, sems.at[n]) for n, (a, b) in enumerate(copies)]
    for copy in copies:
        copy.start()
    for copy in copies:
        copy.wait()


def load(factors, samples, after):
    vmem, hbm = (pl.BlockSpec(memory_space=space) for space in (pltpu.VMEM, pltpu.HBM))
    parts = (samples.shape[0], *samples.shape[2:])
    return pl.pallas_call(
        load_kernel,
        out_shape=[pltpu.VMEM(factors.shape, factors.dtype), pltpu.VMEM(parts, samples.dtype)],
        in_specs=[hbm, hbm] + [vmem] * len(after),
        out_specs=[vmem, vmem],
        scratch_shapes=[pltpu.SemaphoreType.DMA((factors.shape[0] + 1,))],
        compiler_params=pltpu.CompilerParams(vmem_limit_bytes=2**23),
    )(
        *[pltpu.with_memory_space_constraint(value, pltpu.HBM) for value in (factors, samples)],
        *[pltpu.with_memory_space_constraint(value, pltpu.VMEM) for value in after],
    )


def cast_kernel(image_ref, out_ref):
    flat = image_ref[...].reshape(out_ref.shape[1], out_ref.shape[0])
    out_ref[...] = flat.T.astype(BF16)


def near_kernel(mask_ref, *refs):
    pieces, (v_ref, near_ref, held) = refs[:-3], refs[-3:]
    count, col_tiles = len(pieces), v_ref.shape[1]
    me_row = lax.axis_index("row")
    tile = me_row // count
    for distance in range(count):
        held[(me_row % count) ^ distance] = pieces[distance][...]
    lhs = jnp.concatenate([held[p] for p in range(count)], axis=1)
    for i in range(v_ref.shape[0]):
        value = jnp.dot(lhs, v_ref[i, tile], preferred_element_type=F32)
        near_ref[i] = (value * mask_ref[pl.ds(i * col_tiles + tile, 1)]).astype(BF16)


def half_rows(u_ref, coef_ref, i, low, core):
    total = None
    for j in range(u_ref.shape[1]):
        rows = u_ref[low + i, j, :, core]
        rows = rows.reshape(rows.shape[0] * rows.shape[1], rows.shape[2])
        term = dot_nt(rows, coef_ref[i, j])
        total = term if total is None else total + term
    return total.reshape(u_ref.shape[2], u_ref.shape[4], total.shape[1])


def forward_kernel(low, mask_ref, near_ref, *refs):
    pieces, (u_ref, v_ref, cross_ref, coef_ref, held) = refs[:-5], refs[-5:]
    col_tiles, chips = u_ref.shape[1:3]
    per_tile = len(pieces) // (col_tiles - 1)
    me_row, me_col = lax.axis_index("row"), lax.axis_index("col")
    own_tile = me_row // per_tile
    for n, piece in enumerate(pieces, per_tile):
        held[me_row ^ n] = piece[...]
    for i in range(coef_ref.shape[0]):
        coef_ref[i, own_tile] = near_ref[low + i]
    for n in range(1, col_tiles):
        tile = own_tile ^ n
        lhs = jnp.concatenate([held[tile * per_tile + p] for p in range(per_tile)], axis=1)
        for i in range(coef_ref.shape[0]):
            value = jnp.dot(lhs, v_ref[low + i, tile], preferred_element_type=F32)
            value = value * mask_ref[pl.ds((low + i) * col_tiles + tile, 1)]
            coef_ref[i, tile] = value.astype(BF16)
    chip, core = me_col // 2, me_col % 2
    for i in range(coef_ref.shape[0]):
        value = half_rows(u_ref, coef_ref, i, low, 1 - core)
        for q in range(chips):
            cross_ref[chip ^ q, i] = value[q].astype(cross_ref.dtype)


def own_kernel(low, coef_ref, u_ref, mine_ref):
    me_col = lax.axis_index("col")
    chip, core = me_col // 2, me_col % 2
    for i in range(coef_ref.shape[0]):
        value = half_rows(u_ref, coef_ref, i, low, core)
        for q in range(u_ref.shape[2]):
            mine_ref[chip ^ q, i] = value[q]


def sum_kernel(low, mine_ref, crossed_ref, wanted_ref, own_ref, *send_refs):
    value = mine_ref[0] + crossed_ref[0].astype(F32)
    own_ref[...] = value - wanted_ref[pl.ds(low, own_ref.shape[0])].astype(F32)
    for q, send_ref in enumerate(send_refs, 1):
        send_ref[...] = (mine_ref[q] + crossed_ref[q].astype(F32)).astype(BF16)


def resid_kernel(own_ref, *refs):
    out_ref = refs[-1]
    for i in range(own_ref.shape[0]):
        value = own_ref[i]
        for ref in refs[:-1]:
            value = value + ref[i].astype(F32)
        out_ref[i] = value.T.astype(BF16)


def hold(held, pieces):
    me_col = lax.axis_index("col")
    for distance, piece in enumerate(pieces):
        held[me_col ^ distance] = piece[...]


def back_tile(held, mask_ref, u_ref, tile, i, low):
    count, col_tiles = held.shape[0], u_ref.shape[1]
    lhs = jnp.concatenate([held[p, i] for p in range(count)], axis=1)
    value = jnp.dot(lhs, u_ref[low + i, tile], preferred_element_type=F32)
    return (value * mask_ref[pl.ds((low + i) * col_tiles + tile, 1)]).astype(BF16)


def back_kernel(mask_ref, *refs):
    pieces, (u_ref, back_ref, held) = refs[:-3], refs[-3:]
    hold(held, pieces)
    for i in range(back_ref.shape[0]):
        for tile in range(u_ref.shape[1]):
            back_ref[i, tile] = back_tile(held, mask_ref, u_ref, tile, i, 0)


def adjoint_kernel(count, brick, distances, mask_ref, early_ref, *refs):
    pieces, (u_ref, v_ref), rest = refs[:count], refs[count : count + 2], refs[count + 2 :]
    outs, (held, back_ref) = rest[:-2], rest[-2:]
    row_tiles, tile_len = u_ref.shape[0], u_ref.shape[2]
    low, size = early_ref.shape[0], outs[0].shape[0]
    per_tile, cuts = tile_len // brick, brick // size
    me_row = lax.axis_index("row")
    hold(held, pieces)
    ready = None
    for n, distance in enumerate(distances):
        tile = (me_row // per_tile) ^ (distance // per_tile)
        if ready != distance // per_tile:
            ready = distance // per_tile
            for i in range(row_tiles - low):
                back_ref[i] = back_tile(held, mask_ref, u_ref, tile, i, low)
        for cut in range(cuts):
            inside = ((me_row % per_tile) ^ (distance % per_tile)) * brick + cut * size
            inside = pl.multiple_of(inside, size)
            value = None
            for i in range(row_tiles):
                back = early_ref[i, tile] if i < low else back_ref[i - low]
                term = dot_nt(v_ref[i, tile, pl.ds(inside, size)], back)
                value = term if value is None else value + term
            out_ref = outs[n * cuts + cut]
            out_ref[...] = value.astype(out_ref.dtype)


def add_kernel(part_ref, *refs):
    value = part_ref[...]
    for ref in refs[:-1]:
        value = value + ref[...].astype(F32)
    refs[-1][...] = value.astype(BF16)


def move_kernel(cuts, image_ref, *refs):
    parts, (moved_ref, even_ref, odd_ref, side_ref) = refs[:-4], refs[-4:]
    terms = []
    for cut in range(cuts):
        value = parts[cut][...]
        for ref in parts[cuts + cut :: cuts]:
            value = value + ref[...].astype(F32)
        terms.append(value)
    gradient = jnp.concatenate(terms, axis=0)
    moved = image_ref[...] - gradient.reshape(image_ref.shape)
    moved_ref[...] = moved
    side_ref[...] = moved.astype(BF16)
    width = even_ref.shape[0]
    far = image_ref.shape[0] - width
    odd = lax.axis_index("row") % 2
    even_ref[...] = moved_ref[pl.ds((1 - odd) * far, width)].astype(BF16)
    odd_ref[...] = moved_ref[pl.ds(odd * far, width)].astype(BF16)


def corner_kernel(even_ref, odd_ref, to_even_ref, to_odd_ref):
    last = even_ref.shape[1] - 1
    row_odd, col_odd = lax.axis_index("row") % 2, lax.axis_index("col") % 2
    near, side = (1 - col_odd) * last, col_odd * last
    for out_ref, y in ((to_even_ref, near), (to_odd_ref, side)):
        low = jnp.where(row_odd == 1, even_ref[1, y], odd_ref[1, y])
        high = jnp.where(row_odd == 1, odd_ref[0, y], even_ref[0, y])
        out_ref[0] = low
        out_ref[1] = high


def flux(delta):
    scaled = delta / edge_scale
    return delta / (1.0 + scaled * scaled)


def grid_position():
    rows, cols = lax.axis_size("row"), lax.axis_size("col")
    me_row, me_col = lax.axis_index("row"), lax.axis_index("col")
    return me_row, me_col, (me_row > 0, me_row < rows - 1), (me_col > 0, me_col < cols - 1)


def within(value, inside):
    return jnp.where(inside, value.astype(F32), 0.0)


def diffuse(cells, get):
    faces = {}

    def face(kind, x, y):
        key = (kind, x, y)
        if key not in faces:
            x2, y2 = (x + 1, y) if kind == 0 else (x, y + 1)
            faces[key] = flux(get(x2, y2) - get(x, y))
        return faces[key]

    new = {}
    for x, y in cells:
        u = get(x, y)
        depth = u.shape[0]
        level = lax.broadcasted_iota(jnp.int32, u.shape, 0)
        below = jnp.where(level == 0, 0.0, pltpu.roll(u, 1, 0))
        down = flux(u - below)
        up = jnp.where(level == depth - 1, flux(-u), pltpu.roll(down, depth - 1, 0))
        total = face(0, x, y) - face(0, x - 1, y)
        total = total + (face(1, x, y) - face(1, x, y - 1))
        new[x, y] = u + diff_rate * (total + (up - down))
    return new


def inner_kernel(moved_ref, row_even, row_odd, col_even, col_odd, field, fresh_ref):
    nx, ny = moved_ref.shape[:2]
    me_row, me_col, (low_x, high_x), (low_y, high_y) = grid_position()
    r_odd, c_odd = me_row % 2, me_col % 2
    field[2 : 2 + nx, 2 : 2 + ny] = moved_ref[...]
    far_x, far_y = nx + 2, ny + 2
    field[pl.ds((1 - r_odd) * far_x, 2), 2 : 2 + ny] = row_even[...].astype(F32)
    field[pl.ds(r_odd * far_x, 2), 2 : 2 + ny] = within(row_odd[...], low_x & high_x)
    field[2 : 2 + nx, pl.ds((1 - c_odd) * far_y, 2)] = col_even[...].astype(F32)
    field[2 : 2 + nx, pl.ds(c_odd * far_y, 2)] = within(col_odd[...], low_y & high_y)
    cells = [(x, y) for x in range(2, 2 + nx) for y in range(2, 2 + ny)]
    for (x, y), value in diffuse(cells, lambda x, y: field[x, y]).items():
        fresh_ref[x - 2, y - 2] = value


def outer_kernel(field, fresh_ref, corner_even, corner_odd, out_ref, corners, middle, ready, sems):
    nx, ny = fresh_ref.shape[:2]
    me_row, me_col, (low_x, high_x), (low_y, high_y) = grid_position()
    c_odd = me_col % 2
    for side, ref, inside in (
        (1 - c_odd, corner_even, True),
        (c_odd, corner_odd, low_y & high_y),
    ):
        corners[0, side] = within(ref[0], low_x & inside)
        corners[1, side] = within(ref[1], high_x & inside)
    ends_x, ends_y = (1, nx + 2), (1, ny + 2)

    def get(x, y):
        if x in ends_x and y in ends_y:
            return corners[ends_x.index(x), ends_y.index(y)]
        return field[x, y]

    ring = [(x, y) for x in ends_x for y in range(2, 2 + ny)]
    ring += [(x, y) for x in range(2, 2 + nx) for y in ends_y]
    opens = {**dict(zip([("x", x) for x in ends_x], (low_x, high_x)))}
    opens.update(dict(zip([("y", y) for y in ends_y], (low_y, high_y))))
    for (x, y), value in diffuse(ring, get).items():
        inside = opens["x", x] if x in ends_x else opens["y", y]
        middle[x, y] = jnp.where(inside, value, 0.0)

    def later(x, y):
        if 2 <= x < 2 + nx and 2 <= y < 2 + ny:
            return fresh_ref[x - 2, y - 2]
        return middle[x, y]

    cells = [(x, y) for x in range(2, 2 + nx) for y in range(2, 2 + ny)]
    copies = []
    for (x, y), value in diffuse(cells, later).items():
        ready[x - 2, y - 2] = value
        if y == ny + 1:
            copies.append(pltpu.make_async_copy(ready.at[x - 2], out_ref.at[x - 2], sems.at[x - 2]))
            copies[-1].start()
    for copy in copies:
        copy.wait()


def finish(field, fresh, corner_even, corner_odd):
    nx, ny, depth, frames = fresh.shape
    vmem = pl.BlockSpec(memory_space=pltpu.VMEM)
    arrays = (field, fresh, corner_even, corner_odd)
    return pl.pallas_call(
        outer_kernel,
        name="outer",
        out_shape=jax.ShapeDtypeStruct(fresh.shape, F32),
        in_specs=[vmem] * 4,
        out_specs=pl.BlockSpec(memory_space=pltpu.HBM),
        scratch_shapes=[
            pltpu.VMEM((2, 2, depth, frames), F32),
            pltpu.VMEM((nx + 4, ny + 4, depth, frames), F32),
            pltpu.VMEM(fresh.shape, F32),
            pltpu.SemaphoreType.DMA((nx,)),
        ],
        compiler_params=pltpu.CompilerParams(vmem_limit_bytes=2**23),
    )(*[pltpu.with_memory_space_constraint(value, pltpu.VMEM) for value in arrays])


def step(image, u_factors, v_factors, ranks, measured):
    row_tiles, col_tiles, tile_len, rank_max = u_factors.shape
    nx, ny, depth, frames = image.shape
    brick = nx * ny * depth
    per_tile = tile_len // brick
    rows, cols = lax.axis_size("row"), lax.axis_size("col")
    chips, part_len = cols // 2, tile_len // cols
    level = lax.broadcasted_iota(jnp.int32, (row_tiles * col_tiles, rank_max), 1)
    mask = (level < ranks.reshape(-1, 1)).astype(F32)
    samples = measured.reshape(row_tiles, cols, part_len, frames)

    own_x = call(cast_kernel, (image,), [((frames, brick), BF16)])[0]
    have = {0: own_x}
    for bit in reversed(bits_of(rows)):
        for distance in list(have):
            have[distance ^ bit] = swap(have[distance], "row", bit)
    pieces = [have[distance] for distance in range(rows)]
    v_factors, wanted = load(v_factors, samples, (own_x, mask))
    u_factors, _ = load(u_factors, samples, (own_x, mask))

    u_factors = u_factors.reshape(row_tiles, col_tiles, chips, 2, part_len, rank_max)
    split = (row_tiles + 1) // 2
    groups = [(0, split), (split, row_tiles - split)]
    near, v_factors = call(
        near_kernel,
        (mask, *pieces[:per_tile], v_factors),
        [((row_tiles, frames, rank_max), BF16)],
        [pltpu.VMEM((per_tile, frames, brick), BF16)],
        through=1,
    )
    crossed, mine = [], []
    for low, size in groups:
        half = (chips, size, part_len, frames)
        cross, coef, u_factors, v_factors = call(
            functools.partial(forward_kernel, low),
            (mask, near, *pieces[per_tile:], u_factors, v_factors),
            [(half, BF16), ((size, col_tiles, frames, rank_max), BF16)],
            [pltpu.VMEM((rows, frames, brick), BF16)],
            through=2,
        )
        crossed.append(swap(cross, "col", 1))
        value, u_factors = call(
            functools.partial(own_kernel, low), (coef, u_factors), [(half, F32)], through=1
        )
        mine.append(value)
    u_factors = u_factors.reshape(row_tiles, col_tiles, tile_len, rank_max)
    own, received = [], []
    for n, (low, size) in enumerate(groups):
        part = (size, part_len, frames)
        value, *sends = call(
            functools.partial(sum_kernel, low),
            (mine[n], crossed[n], wanted),
            [(part, F32)] + [(part, BF16)] * (chips - 1),
        )
        own.append(value)
        received.append([])
        for q, value in enumerate(sends, 1):
            received[n].append(swap(value, "col", 2 * q))
    parts = []
    for n, (low, size) in enumerate(groups):
        (resid,) = call(resid_kernel, (own[n], *received[n]), [((size, frames, part_len), BF16)])
        pieces = {}
        for q in range(chips):
            pieces[2 * q] = swap(resid, "col", 2 * q) if q else resid
            pieces[2 * q + 1] = swap(pieces[2 * q], "col", 1)
        parts.append([pieces[d] for d in range(cols)])
    size = groups[0][1]
    early, u_factors = call(
        back_kernel,
        (mask, *parts[0], u_factors),
        [((size, col_tiles, frames, rank_max), BF16)],
        [pltpu.VMEM((cols, size, frames, part_len), BF16)],
        through=1,
    )

    cuts = 1

    def adjoint(distances, u_factors, v_factors):
        size = groups[1][1]
        kinds = [BF16 if d % 2 else F32 for d in distances for _ in range(cuts)]
        *terms, u_factors, v_factors = call(
            functools.partial(adjoint_kernel, cols, brick, distances),
            (mask, early, *parts[1], u_factors, v_factors),
            [((brick // cuts, frames), kind) for kind in kinds],
            [
                pltpu.VMEM((cols, size, frames, part_len), BF16),
                pltpu.VMEM((size, frames, rank_max), BF16),
            ],
            through=2,
        )
        for n, d in enumerate(distances):
            pieces[d] = terms[n * cuts : (n + 1) * cuts]
        return u_factors, v_factors

    pieces, sums = {}, {}
    u_factors, v_factors = adjoint(list(range(3, rows, 2)), u_factors, v_factors)
    for d in range(3, rows, 2):
        for cut in range(cuts):
            sums[d - 1, cut] = [swap(pieces[d][cut], "row", 1)]
    rest = [*range(2, rows, 2), 1, 0]
    u_factors, v_factors = adjoint(rest, u_factors, v_factors)
    for cut in range(cuts):
        sums[0, cut] = [swap(pieces[1][cut], "row", 1)]
    for bit in bits_of(rows)[1:]:
        for d in range(bit, rows, 2 * bit):
            for cut in range(cuts):
                (value,) = call(
                    add_kernel, (pieces[d][cut], *sums[d, cut]), [(pieces[d][cut].shape, BF16)]
                )
                sums[d ^ bit, cut].append(swap(value, "row", bit))
    terms = [*zip(*[sums[0, cut] for cut in range(cuts)])]
    terms = [*pieces[0], *[value for pair in terms for value in pair]]

    edge = (2, ny, depth, frames)
    moved, to_even, to_odd, side = call(
        functools.partial(move_kernel, cuts),
        (image, *terms),
        [(image.shape, F32), (edge, BF16), (edge, BF16), (image.shape, BF16)],
    )
    row_even = swap(to_even, "row", 1)
    row_odd = swap_odd(to_odd, "row")
    col_odd = swap_odd(side, "col")
    col_even = swap(side, "col", 1)
    corner = (2, depth, frames)
    to_even, to_odd = call(corner_kernel, (row_even, row_odd), [(corner, BF16)] * 2)
    corner_odd = swap_odd(to_odd, "col")
    corner_even = swap(to_even, "col", 1)
    field, fresh = call(
        inner_kernel,
        (moved, row_even, row_odd, col_even, col_odd),
        [((nx + 4, ny + 4, depth, frames), F32), (image.shape, F32)],
    )
    return finish(field, fresh, corner_even, corner_odd)


def solution(mesh):
    placed = (
        P("row", "col", None, None),
        P("row", "col", None, None),
        P("row", "col", None, None),
        P("row", "col"),
        P("row", None),
    )
    return jax.shard_map(
        step, mesh=mesh, in_specs=placed, out_specs=P("row", "col", None, None), check_vma=False
    )
```
